32 devices in a mesh: layer: 2 (over x), row: 16 (over z, y, core).
Axes of the slice: x: 2, y: 2, z: 4, core: 2. Of those that a mesh axis runs over, the one named last changes fastest.
Arguments:
- leaf_rhs: float32 [2, 16, 256, 384], P('layer', 'row'), may hold values from -6 to 6
- leaf_inverse: float32 [2, 16, 256, 256], P('layer', 'row'), may hold values from -0.375 to 0.375
- leaf_coupling: float32 [2, 16, 4, 512, 256], P('layer', 'row'), may hold values from -0.09375 to 0.09375
- parent: int32 [2, 16], P('layer', 'row'), may hold values from 0 to 3
- sep_rhs: float32 [2, 4, 512, 384], P('layer', None, 'row'), may hold values from -6 to 6
- sep_inverse: float32 [2, 4, 512, 512], P('layer', None, 'row'), may hold values from -0.25 to 0.25
- sep_coupling: float32 [2, 3, 512, 512], P('layer', None, 'row'), may hold values from -0.125 to 0.125
- root_coupling: float32 [2, 512, 512], P('layer', 'row'), may hold values from -0.1875 to 0.1875
- root_rhs: float32 [512, 384], P('row'), may hold values from -6 to 6
- root_inverse: float32 [512, 512], P('row'), may hold values from -0.25 to 0.25
Outputs:
- sep_solution: float32 [2, 4, 512, 384], P('layer', None, 'row')
- root_solution: float32 [512, 384], P('row')
The draws below stay inside these ranges and needn't reach their ends.
All inputs are finite; a program needn't handle non-finite values.
Results may differ from the reference program's by a relative error of at most 0.0003.
Values sent between devices are 32-bit elements; how exact they have to be, the bound alone decides.
A program may use at most 64 MiB of HBM per device.

```python
import jax
import jax.numpy as jnp
from jax import lax

W = 512
SEPS = 4
LEAF = 256
R = 384
N_LAYER = 2
N_ROW = 16


def with_ends(array, own_key, low, largest):
    index_at = [jax.random.randint(jax.random.fold_in(own_key, axis), (), 0, length) for axis, length in enumerate(array.shape)]
    widest = array.shape.index(max(array.shape))
    beside = index_at[:widest] + [(index_at[widest] + 1) % array.shape[widest]] + index_at[widest + 1:]
    return array.at[tuple(index_at)].set(low).at[tuple(beside)].set(largest)


def block_levels(rng, dims, shards, low, largest):
    def one(position, shards_of):
        steps = jax.random.uniform(jax.random.fold_in(jax.random.fold_in(rng, 6), position), (shards_of,), jnp.float32, low / len(shards), largest / len(shards))
        return jnp.repeat(jnp.exp(steps), dims[position] // shards_of).reshape((-1,) + (1,) * (len(dims) - position - 1))

    factor_of = one(*shards[0])
    for cut in shards[1:]:
        factor_of = factor_of * one(*cut)
    return factor_of


def normal_values(own_key, shape, scale, bound, cuts=(), kind=jnp.bfloat16):
    factor_of = block_levels(own_key, shape, cuts, -0.22, 0.18) if cuts else 1.0
    values = jax.random.normal(own_key, shape, jnp.float32) * scale * factor_of
    return jnp.minimum(jnp.maximum(values, -bound), bound).astype(kind)


def setup_inputs(seed: int = 0) -> dict:
    seeds = jax.random.split(jax.random.key(seed), 11)
    return {
        "leaf_rhs": normal_values(seeds[0], (N_LAYER, N_ROW, LEAF, R), 1.0, 6.0, ((0, 2), (1, 16)), jnp.float32),
        "leaf_inverse": normal_values(seeds[1], (N_LAYER, N_ROW, LEAF, LEAF), LEAF ** -0.5, 0.375, ((0, 2), (1, 16)), jnp.float32),
        "leaf_coupling": normal_values(seeds[2], (N_LAYER, N_ROW, SEPS, W, LEAF), (LEAF * N_ROW) ** -0.5, 0.09375, ((0, 2), (1, 16)), jnp.float32),
        "parent": with_ends(jax.random.randint(seeds[3], (N_LAYER, N_ROW), 0, SEPS), jax.random.fold_in(seeds[3], 1), 0, SEPS - 1).astype(jnp.int32),
        "sep_rhs": normal_values(seeds[4], (N_LAYER, SEPS, W, R), 1.0, 6.0, ((0, 2), (2, 16)), jnp.float32),
        "sep_inverse": normal_values(seeds[5], (N_LAYER, SEPS, W, W), W ** -0.5, 0.25, ((0, 2), (2, 16)), jnp.float32),
        "sep_coupling": normal_values(seeds[6], (N_LAYER, SEPS - 1, W, W), (4 * W) ** -0.5, 0.125, ((0, 2), (2, 16)), jnp.float32),
        "root_coupling": normal_values(seeds[7], (N_LAYER, W, W), (W * N_LAYER) ** -0.5, 0.1875, ((0, 2), (1, 16)), jnp.float32),
        "root_rhs": normal_values(seeds[8], (W, R), 1.0, 6.0, ((0, 16),), jnp.float32),
        "root_inverse": normal_values(seeds[9], (W, W), W ** -0.5, 0.25, ((0, 16),), jnp.float32),
    }


def reference(leaf_rhs, leaf_inverse, leaf_coupling, parent, sep_rhs, sep_inverse, sep_coupling, root_coupling, root_rhs, root_inverse):
    highest = lax.Precision.HIGHEST

    def one_layer(inputs):
        rhs_layer, inverse_layer, coupling_layer, parent_layer, sep_rhs_layer, sep_inverse_layer, chain_layer = inputs
        leaf_solution = jnp.einsum('rab,rbc->rac', inverse_layer, rhs_layer, precision=highest)
        levels = jnp.arange(SEPS, dtype=jnp.int32)
        keep_mask = (levels[None, :] >= parent_layer[:, None]).astype(jnp.float32)
        coupled = jnp.einsum('rkwb,rbc,rk->kwc', coupling_layer, leaf_solution, keep_mask, precision=highest)
        residual = sep_rhs_layer - coupled
        solved = []
        previous = None
        for k in range(SEPS):
            current = jnp.dot(sep_inverse_layer[k], residual[k], precision=highest)
            if k > 0:
                current = current - jnp.dot(chain_layer[k - 1], previous, precision=highest)
            solved.append(current)
            previous = current
        return jnp.stack(solved)

    sep_solution = lax.map(one_layer, (leaf_rhs, leaf_inverse, leaf_coupling, parent, sep_rhs, sep_inverse, sep_coupling))
    root_update = jnp.einsum('lwv,lvc->wc', root_coupling, sep_solution[:, SEPS - 1], precision=highest)
    root_residual = root_rhs - root_update
    root_solution = jnp.dot(root_inverse, root_residual, precision=highest)
    return sep_solution, root_solution
```

```python
import functools

import jax
import jax.numpy as jnp
from jax import lax
from jax.experimental import pallas as pl
from jax.experimental.pallas import tpu as pltpu
from jax.sharding import PartitionSpec as P

MESH = pl.DeviceIdType.MESH
NN = (((1,), (0,)), ((), ()))
NT = (((1,), (1,)), ((), ()))
HALVES = 2
LAG = 2
BEFORE = 1
SHIFT = (0, 0, 0, 0)


def split(a):
    high = a.astype(jnp.bfloat16)
    return high, (a - high.astype(jnp.float32)).astype(jnp.bfloat16)


def dot3(a, b, dims):
    (ah, al), (bh, bl) = a, b
    dot = functools.partial(lax.dot_general, dimension_numbers=dims, preferred_element_type=jnp.float32)
    return dot(ah, bh) + (dot(ah, bl) + dot(al, bh))


def kernel(
    n_z,
    parent,
    leaf_rhs,
    leaf_inverse,
    leaf_coupling,
    sep_rhs,
    sep_inverse,
    sep_coupling,
    root_coupling,
    root_rhs,
    root_inverse,
    sep_out,
    root_out,
    v_rhs,
    v_inv,
    v_coup,
    v_sep,
    g_inv,
    g_chain,
    g_rc,
    g_rr,
    g_ri,
    part,
    from_core,
    to_y,
    from_y,
    mine,
    fwd,
    bwd,
    from_left,
    from_right,
    total,
    solved,
    padded,
    turned,
    pieces,
    root_send,
    root_recv,
    root_full,
    load,
    own_load,
    w_send,
    w_recv,
    c_send,
    c_recv,
    y_send,
    y_recv,
    f_send,
    f_recv,
    b_send,
    b_recv,
    a_send,
    a_recv,
    o_send,
    o_recv,
    x_send,
    x_recv,
):
    seps, rows, right = v_sep.shape
    width = v_coup.shape[1]
    zrows = width // n_z
    half, quarter = right // 2, right // 4
    sub = quarter // HALVES
    last = seps - 1

    layer = lax.axis_index("layer")
    me = lax.axis_index("row")
    z, y, c = me // 4, (me // 2) % 2, me % 2
    plane = 2 * y + c

    def at(zz, yy, cc):
        return (layer, 4 * zz + 2 * yy + cc)

    core_peer = at(z, y, 1 - c)
    y_peer = at(z, 1 - y, c)
    far_peer = at(z, 1 - y, 1 - c)
    x_peer = (1 - layer, me)
    left, right_peer = (layer, me - 4), (layer, me + 4)
    z_peers = [at((z + d) % n_z, y, c) for d in range(1, n_z)]
    plane_peers = [core_peer, y_peer, far_peer]

    def remote(src, dst, send, recv, peer):
        return pltpu.make_async_remote_copy(
            src_ref=src, dst_ref=dst, send_sem=send, recv_sem=recv, device_id=peer, device_id_type=MESH
        )

    barrier = pltpu.get_barrier_semaphore()
    peers = plane_peers + z_peers + [x_peer]
    for peer in peers:
        pl.semaphore_signal(barrier, inc=1, device_id=peer, device_id_type=MESH)

    own_rows = pl.ds(pl.multiple_of(plane * rows, rows), rows)
    y_rows = pl.ds(pl.multiple_of((2 * (1 - y) + c) * rows, rows), rows)
    weights = [(sep_inverse.at[k], g_inv.at[k]) for k in range(seps)]
    weights += [(sep_coupling.at[k], g_chain.at[k]) for k in range(last)]
    weights += [(root_coupling, g_rc), (root_rhs, g_rr), (root_inverse, g_ri)]
    inv_at, chain_at, rc_at, rr_at, ri_at = 0, seps, seps + last, seps + last + 1, seps + last + 2

    loads = [
        pltpu.make_async_copy(leaf_inverse, v_inv, load.at[0]),
        pltpu.make_async_copy(leaf_rhs, v_rhs, load.at[1]),
        pltpu.make_async_copy(sep_rhs, v_sep, load.at[2]),
    ]
    loads += [pltpu.make_async_copy(leaf_coupling.at[k], v_coup.at[k], load.at[3 + k]) for k in range(seps)]
    for n in (0, 1, 3, 2) + tuple(range(4, 3 + seps)):
        loads[n].start()
    own_loads = [
        pltpu.make_async_copy(source, dest.at[own_rows, :], own_load.at[n])
        for n, (source, dest) in enumerate(weights)
    ]
    for copy in own_loads:
        copy.start()

    def weight(way, n):
        source, dest = weights[n]
        if way == 2:
            source, where = dest.at[y_rows, :], y_rows
        else:
            where = own_rows
        return remote(
            source,
            dest.at[where, :],
            w_send.at[way, n],
            w_recv.at[way, n],
            y_peer if way == 0 else core_peer,
        )

    def relay(n):
        weight(0, n).wait_recv()
        weight(2, n).start()

    def weight_ready(n):
        own_loads[n].wait()
        weight(1, n).wait_recv()
        weight(2, n).wait_recv()

    zlanes = pl.ds(pl.multiple_of(z * zrows, 128), zrows)
    own_y = pl.multiple_of(quarter * y, 8)
    peer_y = pl.multiple_of(quarter * (1 - y), 8)
    padded[...] = jnp.zeros_like(padded)

    def core_copy(k, q):
        there = (peer_y, own_y)[q]
        return remote(
            part.at[k, pl.ds(pl.multiple_of(half * (1 - c) + there, 8), quarter), :],
            from_core.at[k, pl.ds(there, quarter), :],
            c_send.at[k, q],
            c_recv.at[k, q],
            core_peer,
        )

    loads[0].wait()
    loads[1].wait()
    leaf = dot3(split(v_inv[...]), split(v_rhs[...]), NN)
    leaf_t = split(leaf.T)

    def stage_a(k):
        keep = jnp.where(parent[0, 0] <= k, -1.0, 0.0).astype(jnp.float32)
        loads[3 + k].wait()
        part[k] = dot3(leaf_t, split(v_coup[k]), NT) * keep
        if k == 0:
            loads[2].wait()
        padded[own_rows, :] = v_sep[k]
        part[k, :, zlanes] += padded[...].T
        if k == 0:
            pl.semaphore_wait(barrier, len(peers))
            for n in range(BEFORE):
                weight(0, n).start()
        for q in range(2):
            core_copy(k, q).start()

    def y_copy(k, h):
        where = pl.ds(h * sub, sub)
        return remote(
            to_y.at[k, where, :], from_y.at[k, where, :], y_send.at[k, h], y_recv.at[k, h], y_peer
        )

    def stage_b(k):
        core_copy(k, 0).wait_recv()
        to_y[k] = (
            part[k, pl.ds(pl.multiple_of(half * c + peer_y, 8), quarter), :]
            + from_core[k, pl.ds(peer_y, quarter), :]
        )
        for h in range(HALVES):
            y_copy(k, h).start()

    def fwd_copy(k, h):
        where = pl.ds(h * sub, sub)
        return remote(
            fwd.at[k, where, :], from_left.at[k, where, :], f_send.at[k, h], f_recv.at[k, h], right_peer
        )

    def bwd_copy(k, h):
        where = pl.ds(h * sub, sub)
        return remote(
            bwd.at[k, where, :], from_right.at[k, where, :], b_send.at[k, h], b_recv.at[k, h], left
        )

    def stage_c(k, h):
        where = pl.ds(h * sub, sub)
        if h == 0:
            core_copy(k, 1).wait_recv()
        y_copy(k, h).wait_recv()
        mine[k, where, :] = (
            part[k, pl.ds(pl.multiple_of(half * c + own_y + h * sub, 8), sub), :]
            + from_core[k, pl.ds(pl.multiple_of(own_y + h * sub, 8), sub), :]
            + from_y[k, where, :]
        )

    def hop(k, h, number):
        where = pl.ds(h * sub, sub)

        @pl.when(z == number)
        def _():
            if number == 0:
                fwd[k, where, :] = mine[k, where, :]
            else:
                fwd_copy(k, h).wait_recv()
                fwd[k, where, :] = mine[k, where, :] + from_left[k, where, :]
            fwd_copy(k, h).start()

        @pl.when(z == n_z - 1 - number)
        def _():
            if number == 0:
                bwd[k, where, :] = mine[k, where, :]
            else:
                bwd_copy(k, h).wait_recv()
                bwd[k, where, :] = mine[k, where, :] + from_right[k, where, :]
            bwd_copy(k, h).start()

    def finish(k, h):
        where = pl.ds(h * sub, sub)

        @pl.when(z == 0)
        def _():
            bwd_copy(k, h).wait_recv()
            total[k, where, :] = mine[k, where, :] + from_right[k, where, :]

        @pl.when(z == n_z - 1)
        def _():
            fwd_copy(k, h).wait_recv()
            total[k, where, :] = mine[k, where, :] + from_left[k, where, :]

        @pl.when(jnp.logical_and(z > 0, z < n_z - 1))
        def _():
            total[k, where, :] = mine[k, where, :] + (from_left[k, where, :] + from_right[k, where, :])

    def z_lanes(zz):
        return pl.ds(pl.multiple_of(zz * zrows, 128), zrows)

    def along_z(ref, k, h, d, sender):
        where = z_lanes((z - d + n_z) % n_z if sender else z)
        block = ref.at[pl.ds(h * sub, sub), where]
        return remote(block, block, a_send.at[k, h, d - 1], a_recv.at[k, h, d - 1], z_peers[d - 1])

    def out_copy(k, n):
        peer_plane = (2 * y + 1 - c, 2 * (1 - y) + c, 2 * (1 - y) + 1 - c)[n]
        rows_there = pl.ds(pl.multiple_of(peer_plane * rows, rows), rows)
        return remote(
            turned.at[k, rows_there, :], pieces.at[k, n], o_send.at[k, n], o_recv.at[k, n], plane_peers[n]
        )

    def turn(k, value):
        turned[k, :, pl.ds(0, quarter)] = value.T
        for n in range(3):
            out_copy(k, n).start()

    def assemble(k):
        for n in range(3):
            out_copy(k, n).wait_recv()
        own = turned[k, own_rows, :][:, :quarter]
        by_core, by_y, by_far = (pieces[k, n][:, :quarter] for n in range(3))
        low_y, low_core = y == 0, c == 0
        same = (jnp.where(low_y, own, by_y), jnp.where(low_y, by_y, own))
        other = (jnp.where(low_y, by_core, by_far), jnp.where(low_y, by_far, by_core))
        blocks = [jnp.where(low_core, same[n], other[n]) for n in range(2)]
        blocks += [jnp.where(low_core, other[n], same[n]) for n in range(2)]
        return jnp.concatenate(blocks, axis=1)

    def wait_along_z(ref, k, h):
        for d in range(1, n_z):
            along_z(ref, k, h, d, True).wait_recv()

    def send_along_z(ref, k, h):
        for d in range(1, n_z):
            along_z(ref, k, h, d, False).start()

    def chain(k, h):
        where = pl.ds(h * sub, sub)
        if h == 0:
            weight_ready(inv_at + k)
            if k > 0:
                weight_ready(chain_at + k - 1)
        value = dot3(split(total[k, where, :]), split(g_inv[k]), NT)
        if k > 0:
            wait_along_z(solved.at[k - 1], k - 1, h)
            value = value - dot3(split(solved[k - 1, where, :]), split(g_chain[k - 1]), NT)
        solved[k, where, zlanes] = value
        send_along_z(solved.at[k], k, h)
        if h == HALVES - 1:
            turn(k, solved[k, :, zlanes])

    stage_a(0)
    stage_a(1)
    stage_b(0)
    for k in range(2, seps):
        stage_a(k)
        stage_b(k - 1)
    stage_b(last)
    order = [inv_at, inv_at + 1]
    for k in range(1, seps):
        order += [chain_at + k - 1] + [inv_at + k + 1] * (k < last)
    order += [rc_at, rr_at, ri_at]
    for n in order:
        if n >= BEFORE:
            weight(0, n).start()
    for n in order:
        weight(1, n).start()
    chunks = [(k, h) for k in range(seps) for h in range(HALVES)]
    end = len(chunks) + LAG * (n_z - 1)
    relays = {}
    for i, n in enumerate(order):
        relays.setdefault(2 if n < BEFORE else len(chunks) - 1 + (2 * (i + 1 - BEFORE) * HALVES) // 6, []).append(n)
    chains = {}
    for j, (k, h) in enumerate(chunks):
        chains.setdefault(j + LAG * (n_z - 1) + SHIFT[min(k, 3)], []).append((k, h))

    for step in range(max(end, max(chains) + 1)):
        for n in relays.pop(step, []):
            relay(n)
        for number in reversed(range(n_z - 1)):
            j = step - LAG * number
            if 0 <= j < len(chunks):
                if number == 0:
                    stage_c(*chunks[j])
                hop(*chunks[j], number)
        j = step - LAG * (n_z - 1)
        if 0 <= j < len(chunks):
            finish(*chunks[j])
        for k, h in chains.get(step, []):
            chain(k, h)
    for step in sorted(relays):
        for n in relays[step]:
            relay(n)

    for n in range(rc_at, ri_at + 1):
        weight_ready(n)
    root_rhs_t = g_rr[...].T
    turned_rr = part.at[0, :, pl.ds(0, zrows)]
    for k in range(seps):
        for q in range(2):
            core_copy(k, q).wait_send()
    turned_rr[...] = root_rhs_t

    def swap(h):
        where = pl.ds(h * sub, sub)
        return remote(root_send.at[where, :], root_recv.at[where, :], x_send.at[h], x_recv.at[h], x_peer)

    for h in range(HALVES):
        where = pl.ds(h * sub, sub)
        wait_along_z(solved.at[last], last, h)
        root_send[where, :] = dot3(split(solved[last, where, :]), split(g_rc[...]), NT)
        swap(h).start()
    for k in range(last):
        sep_out[k] = assemble(k)
    for h in range(HALVES):
        where = pl.ds(h * sub, sub)
        swap(h).wait_recv()
        my_cols = pl.ds(pl.multiple_of(half * c + quarter * y + h * sub, 8), sub)
        root_full[where, zlanes] = part[0, my_cols, pl.ds(0, zrows)] - (root_send[where, :] + root_recv[where, :])
        send_along_z(root_full, seps, h)
    sep_out[last] = assemble(last)
    for h in range(HALVES):
        wait_along_z(root_full, seps, h)
    turn(seps, dot3(split(root_full[...]), split(g_ri[...]), NT))
    root_out[...] = assemble(seps)

    for way in range(3):
        for n in range(len(weights)):
            weight(way, n).wait_send()
    for k, h in chunks:
        y_copy(k, h).wait_send()

        @pl.when(z < n_z - 1)
        def _():
            fwd_copy(k, h).wait_send()

        @pl.when(z > 0)
        def _():
            bwd_copy(k, h).wait_send()

    for k in range(seps + 1):
        ref = solved.at[k] if k < seps else root_full
        for h in range(HALVES):
            for d in range(1, n_z):
                along_z(ref, k, h, d, False).wait_send()
        for n in range(3):
            out_copy(k, n).wait_send()
    for h in range(HALVES):
        swap(h).wait_send()


def fused(
    n_z,
    leaf_rhs,
    leaf_inverse,
    leaf_coupling,
    parent,
    sep_rhs,
    sep_inverse,
    sep_coupling,
    root_coupling,
    root_rhs,
    root_inverse,
):
    seps, rows, right = sep_rhs.shape[1:]
    width = sep_inverse.shape[3]
    deep = leaf_inverse.shape[3]
    zrows, half, quarter = width // n_z, right // 2, right // 4
    f32 = jnp.float32
    dma = pltpu.SemaphoreType.DMA
    vmem = pl.BlockSpec(memory_space=pltpu.VMEM)
    hbm = pl.BlockSpec(memory_space=pl.ANY)
    scratch = [
        (deep, right),
        (deep, deep),
        (seps, width, deep),
        (seps, rows, right),
        (seps, zrows, width),
        (seps - 1, zrows, width),
        (zrows, width),
        (zrows, right),
        (zrows, width),
        (seps, right, width),
        (seps, half, width),
    ]
    scratch += [(seps, quarter, width)] * 9
    scratch += [
        (zrows, right),
        (seps + 1, zrows, 128),
        (seps + 1, 3, rows, 128),
        (quarter, zrows),
        (quarter, zrows),
        (quarter, width),
    ]
    n_w = 2 * seps + 2
    sems = [(3 + seps,), (n_w,)]
    sems += [(3, n_w)] * 2 + [(seps, 2)] * 2 + [(seps, HALVES)] * 6
    sems += [(seps + 1, HALVES, n_z - 1)] * 2 + [(seps + 1, 3)] * 2 + [(HALVES,)] * 2
    sep, root = pl.pallas_call(
        functools.partial(kernel, n_z),
        out_shape=(
            jax.ShapeDtypeStruct((seps, rows, right), f32),
            jax.ShapeDtypeStruct((rows, right), f32),
        ),
        in_specs=[pl.BlockSpec(memory_space=pltpu.SMEM)] + [hbm] * 9,
        out_specs=(vmem, vmem),
        scratch_shapes=[pltpu.VMEM(s, f32) for s in scratch] + [dma(s) for s in sems],
        compiler_params=pltpu.CompilerParams(
            collective_id=0, has_side_effects=True, vmem_limit_bytes=60 * 2**20
        ),
        name="forward_solve",
    )(
        parent,
        leaf_rhs.reshape(leaf_rhs.shape[2:]),
        leaf_inverse.reshape(leaf_inverse.shape[2:]),
        leaf_coupling.reshape(leaf_coupling.shape[2:]),
        sep_rhs.reshape(sep_rhs.shape[1:]),
        sep_inverse.reshape(sep_inverse.shape[1:]),
        sep_coupling.reshape(sep_coupling.shape[1:]),
        root_coupling.reshape(root_coupling.shape[1:]),
        root_rhs,
        root_inverse,
    )
    return sep[None], root


def body(
    leaf_rhs,
    leaf_inverse,
    leaf_coupling,
    parent,
    sep_rhs,
    sep_inverse,
    sep_coupling,
    root_coupling,
    root_rhs,
    root_inverse,
):
    highest = lax.Precision.HIGHEST
    sep_count = sep_rhs.shape[1]
    row_count = sep_rhs.shape[2]
    row_start = lax.axis_index("row") * row_count
    leaf_solution = jnp.dot(leaf_inverse[0, 0], leaf_rhs[0, 0], precision=highest)
    levels = jnp.arange(sep_count, dtype=jnp.int32)
    keep_mask = (levels >= parent[0, 0]).astype(jnp.float32)

    def residual_term(k):
        coupled = jnp.dot(leaf_coupling[0, 0, k], leaf_solution, precision=highest) * keep_mask[k]
        own_rhs = lax.dynamic_update_slice_in_dim(
            jnp.zeros_like(coupled), sep_rhs[0, k], row_start, 0
        )
        return own_rhs - coupled

    residual_list = [lax.psum(residual_term(k), "row") for k in range(sep_count)]
    local_rows = [
        jnp.dot(sep_inverse[0, k], residual_list[k], precision=highest) for k in range(sep_count)
    ]
    solved = []
    gathered = None
    for k in range(sep_count):
        current = local_rows[k]
        if k > 0:
            current = current - jnp.dot(sep_coupling[0, k - 1], gathered, precision=highest)
        solved.append(current)
        gathered = lax.all_gather(current, "row", axis=0, tiled=True)
    sep_out = jnp.stack(solved)[None]
    root_term = jnp.dot(root_coupling[0], gathered, precision=highest)
    root_sum = lax.psum(root_term, "layer")
    root_residual = root_rhs - root_sum
    root_out = jnp.dot(
        root_inverse, lax.all_gather(root_residual, "row", axis=0, tiled=True), precision=highest
    )
    return (sep_out, root_out)


def solution(mesh):
    n_layer, n_row = mesh.shape["layer"], mesh.shape["row"]

    def per_device(*arrays):
        right, width = arrays[0].shape[3], arrays[5].shape[3]
        n_z = n_row // 4
        fits = (
            n_layer == 2
            and n_row in (8, 16)
            and width % (128 * n_z) == 0
            and right % (32 * HALVES) == 0
            and right // 4 <= 128
            and arrays[4].shape[1] >= 3
        )
        return functools.partial(fused, n_z)(*arrays) if fits else body(*arrays)

    return jax.shard_map(
        per_device,
        mesh=mesh,
        in_specs=(
            P("layer", "row", None, None),
            P("layer", "row", None, None),
            P("layer", "row", None, None, None),
            P("layer", "row"),
            P("layer", None, "row", None),
            P("layer", None, "row", None),
            P("layer", None, "row", None),
            P("layer", "row", None),
            P("row", None),
            P("row", None),
        ),
        out_specs=(P("layer", None, "row", None), P("row", None)),
        check_vma=False,
    )
```

```python
import functools
import math

import jax
import jax.numpy as jnp
from jax import lax
from jax.experimental import pallas as pl
from jax.experimental.pallas import tpu as pltpu
from jax.sharding import PartitionSpec as P

MESH = pl.DeviceIdType.MESH
NN = (((1,), (0,)), ((), ()))
NT = (((1,), (1,)), ((), ()))
HALVES = 2
LAG = 2
PLAN = ((0,), (), (1,), (4,), (2, 5, 3, 6, 9, 8))
SHIFT = (0, 0, 1, 2)
JOIN = 13
ROUNDS = (1, 3, 5)


def split(a):
    high = a.astype(jnp.bfloat16)
    return high, (a - high.astype(jnp.float32)).astype(jnp.bfloat16)


def dot3(a, b, dims):
    (ah, al), (bh, bl) = a, b
    dot = functools.partial(lax.dot_general, dimension_numbers=dims, preferred_element_type=jnp.float32)
    return dot(ah, bh) + (dot(ah, bl) + dot(al, bh))


def kernel(
    n_z,
    parent,
    leaf_rhs,
    leaf_inverse,
    leaf_coupling,
    sep_rhs,
    sep_inverse,
    sep_coupling,
    root_coupling,
    root_rhs,
    root_inverse,
    sep_final,
    root_final,
    sep_out,
    root_out,
    v_rhs,
    v_inv,
    v_coup,
    v_sep,
    g_inv,
    g_chain,
    g_m,
    g_q,
    g_rr,
    g_ri,
    part,
    from_core,
    to_y,
    from_y,
    mine,
    fwd,
    bwd,
    from_left,
    from_right,
    total,
    solved,
    padded,
    turned,
    pieces,
    rr_full,
    rr_out,
    root_pieces,
    load,
    own_load,
    w_send,
    w_recv,
    c_send,
    c_recv,
    y_send,
    y_recv,
    f_send,
    f_recv,
    b_send,
    b_recv,
    a_send,
    a_recv,
    o_send,
    o_recv,
    x_send,
    x_recv,
    q_send,
    q_recv,
    m_send,
    m_recv,
    qz_send,
    qz_recv,
    r_send,
    r_recv,
    end,
):
    seps, rows, right = v_sep.shape
    width = v_coup.shape[1]
    zrows = width // n_z
    half, quarter = right // 2, right // 4
    sub = quarter // HALVES
    last = seps - 1

    layer = lax.axis_index("layer")
    me = lax.axis_index("row")
    z, y, c = me // 4, (me // 2) % 2, me % 2
    plane = 2 * y + c

    def at(zz, yy, cc):
        return (layer, 4 * zz + 2 * yy + cc)

    core_peer = at(z, y, 1 - c)
    y_peer = at(z, 1 - y, c)
    far_peer = at(z, 1 - y, 1 - c)
    x_peer = (1 - layer, me)
    lanes = width // 4
    left, right_peer = (layer, me - 4), (layer, me + 4)
    z_peers = [at((z + d) % n_z, y, c) for d in range(1, n_z)]
    plane_peers = [core_peer, y_peer, far_peer]

    def remote(src, dst, send, recv, peer):
        return pltpu.make_async_remote_copy(
            src_ref=src, dst_ref=dst, send_sem=send, recv_sem=recv, device_id=peer, device_id_type=MESH
        )

    barrier = pltpu.get_barrier_semaphore()
    near = plane_peers + [x_peer]
    for peer in near:
        pl.semaphore_signal(barrier, inc=1, device_id=peer, device_id_type=MESH)

    @pl.when(z > 0)
    def _():
        pl.semaphore_signal(barrier, inc=1, device_id=left, device_id_type=MESH)

    @pl.when(z < n_z - 1)
    def _():
        pl.semaphore_signal(barrier, inc=1, device_id=right_peer, device_id_type=MESH)

    def enter():
        pl.semaphore_wait(barrier, len(near) + jnp.minimum(z, 1) + jnp.minimum(n_z - 1 - z, 1))


    own_rows = pl.ds(pl.multiple_of(plane * rows, rows), rows)
    y_rows = pl.ds(pl.multiple_of((2 * (1 - y) + c) * rows, rows), rows)
    weights = [(sep_inverse.at[k], g_inv.at[k]) for k in range(seps)]
    weights += [(sep_coupling.at[k], g_chain.at[k]) for k in range(last)]
    weights += [(root_rhs, g_rr), (root_inverse, g_ri)]
    inv_at, chain_at, rr_at, ri_at = 0, seps, seps + last, seps + last + 1

    loads = [
        pltpu.make_async_copy(leaf_inverse, v_inv, load.at[0]),
        pltpu.make_async_copy(leaf_rhs, v_rhs, load.at[1]),
        pltpu.make_async_copy(sep_rhs, v_sep, load.at[2]),
    ]
    loads += [pltpu.make_async_copy(leaf_coupling.at[k], v_coup.at[k], load.at[3 + k]) for k in range(seps)]
    for n in (0, 1, 3, 2) + tuple(range(4, 3 + seps)):
        loads[n].start()
    own_loads = [
        pltpu.make_async_copy(source, dest.at[own_rows, :], own_load.at[n])
        for n, (source, dest) in enumerate(weights)
    ]
    my_lanes = pl.ds(pl.multiple_of(plane * lanes, 128), lanes)
    q_rows = pl.ds(pl.multiple_of(z * zrows + plane * rows, rows), rows)
    z_rows = pl.ds(pl.multiple_of(z * zrows, rows), zrows)
    own_quarter = pltpu.make_async_copy(root_coupling.at[:, my_lanes], g_q.at[q_rows, :], load.at[3 + seps])
    for copy in own_loads + [own_quarter]:
        copy.start()

    plane_of = (2 * y + 1 - c, 2 * (1 - y) + c, 2 * (1 - y) + 1 - c)

    def quarter_copy(n):
        there = pl.ds(pl.multiple_of(plane_of[n] * lanes, 128), lanes)
        return remote(
            root_coupling.at[:, there], g_q.at[q_rows, :], q_send.at[n], q_recv.at[n], plane_peers[n]
        )

    def quarter_hop(side, number, sent):
        owner = (z - number, z + number)[side] if sent else (z - 1 - number, z + 1 + number)[side]
        block = g_q.at[pl.ds(pl.multiple_of(owner * zrows, rows), zrows), :]
        return remote(
            block, block, qz_send.at[side, number], qz_recv.at[side, number], (right_peer, left)[side]
        )

    def takes(side, number):
        return (z - 1 - number >= 0, z + 1 + number < n_z)[side]

    def gives(side, number):
        far = (z - number >= 0, z + number < n_z)[side]
        return jnp.logical_and(far, (z < n_z - 1, z > 0)[side])

    def quarter_round(number):
        for side in range(2):
            if number > 0:

                @pl.when(takes(side, number - 1))
                def _():
                    quarter_hop(side, number - 1, False).wait_recv()

            if number < n_z - 1:

                @pl.when(gives(side, number))
                def _():
                    quarter_hop(side, number, True).start()

    def product_copy(n):
        return remote(
            g_m.at[:, my_lanes], g_m.at[:, my_lanes], m_send.at[n], m_recv.at[n], plane_peers[n]
        )

    def send_weights(place):
        for n in PLAN[place]:
            weight(0, numbers[n]).start()

    numbers = tuple(range(seps + last)) + (None, rr_at, ri_at)

    def weight(way, n):
        source, dest = weights[n]
        if way == 2:
            source, where = dest.at[y_rows, :], y_rows
        else:
            where = own_rows
        return remote(
            source,
            dest.at[where, :],
            w_send.at[way, n],
            w_recv.at[way, n],
            y_peer if way == 0 else core_peer,
        )

    def relay(n):
        weight(0, n).wait_recv()
        weight(2, n).start()

    def weight_ready(n):
        own_loads[n].wait()
        weight(1, n).wait_recv()
        weight(2, n).wait_recv()

    zlanes = pl.ds(pl.multiple_of(z * zrows, 128), zrows)
    own_y = pl.multiple_of(quarter * y, 8)
    peer_y = pl.multiple_of(quarter * (1 - y), 8)
    padded[...] = jnp.zeros_like(padded)

    def core_copy(k, q):
        there = (peer_y, own_y)[q]
        return remote(
            part.at[k, pl.ds(pl.multiple_of(half * (1 - c) + there, 8), quarter), :],
            from_core.at[k, pl.ds(there, quarter), :],
            c_send.at[k, q],
            c_recv.at[k, q],
            core_peer,
        )

    loads[0].wait()
    loads[1].wait()
    leaf = dot3(split(v_inv[...]), split(v_rhs[...]), NN)
    leaf_t = split(leaf.T)

    share = quarter // 2
    rr_start = pl.multiple_of(half * c + quarter * y + share * layer, 8)
    rr_cols = pl.ds(rr_start, share)

    def stage_a(k):
        keep = jnp.where(parent[0, 0] <= k, -1.0, 0.0).astype(jnp.float32)
        loads[3 + k].wait()
        part[k] = dot3(leaf_t, split(v_coup[k]), NT) * keep
        if k == 0:
            loads[2].wait()
        padded[own_rows, :] = v_sep[k]
        part[k, :, zlanes] += padded[...].T
        if k == 0:
            enter()
            for n in range(3):
                quarter_copy(n).start()
            send_weights(0)
        for q in range(2):
            core_copy(k, q).start()

    def y_copy(k, h):
        where = pl.ds(h * sub, sub)
        return remote(
            to_y.at[k, where, :], from_y.at[k, where, :], y_send.at[k, h], y_recv.at[k, h], y_peer
        )

    def stage_b(k):
        core_copy(k, 0).wait_recv()
        to_y[k] = (
            part[k, pl.ds(pl.multiple_of(half * c + peer_y, 8), quarter), :]
            + from_core[k, pl.ds(peer_y, quarter), :]
        )
        for h in range(HALVES):
            y_copy(k, h).start()

    def fwd_copy(k, h):
        where = pl.ds(h * sub, sub)
        return remote(
            fwd.at[k, where, :], from_left.at[k, where, :], f_send.at[k, h], f_recv.at[k, h], right_peer
        )

    def bwd_copy(k, h):
        where = pl.ds(h * sub, sub)
        return remote(
            bwd.at[k, where, :], from_right.at[k, where, :], b_send.at[k, h], b_recv.at[k, h], left
        )

    def stage_c(k, h):
        where = pl.ds(h * sub, sub)
        if h == 0:
            core_copy(k, 1).wait_recv()
        y_copy(k, h).wait_recv()
        mine[k, where, :] = (
            part[k, pl.ds(pl.multiple_of(half * c + own_y + h * sub, 8), sub), :]
            + from_core[k, pl.ds(pl.multiple_of(own_y + h * sub, 8), sub), :]
            + from_y[k, where, :]
        )

    def hop(k, h, number):
        where = pl.ds(h * sub, sub)

        @pl.when(z == number)
        def _():
            if number == 0:
                fwd[k, where, :] = mine[k, where, :]
            else:
                fwd_copy(k, h).wait_recv()
                fwd[k, where, :] = mine[k, where, :] + from_left[k, where, :]
            fwd_copy(k, h).start()

        @pl.when(z == n_z - 1 - number)
        def _():
            if number == 0:
                bwd[k, where, :] = mine[k, where, :]
            else:
                bwd_copy(k, h).wait_recv()
                bwd[k, where, :] = mine[k, where, :] + from_right[k, where, :]
            bwd_copy(k, h).start()

    def finish(k, h):
        where = pl.ds(h * sub, sub)

        @pl.when(z == 0)
        def _():
            bwd_copy(k, h).wait_recv()
            total[k, where, :] = mine[k, where, :] + from_right[k, where, :]

        @pl.when(z == n_z - 1)
        def _():
            fwd_copy(k, h).wait_recv()
            total[k, where, :] = mine[k, where, :] + from_left[k, where, :]

        @pl.when(jnp.logical_and(z > 0, z < n_z - 1))
        def _():
            total[k, where, :] = mine[k, where, :] + (from_left[k, where, :] + from_right[k, where, :])

    def z_lanes(zz):
        return pl.ds(pl.multiple_of(zz * zrows, 128), zrows)

    def along_z(ref, k, h, d, sender):
        where = z_lanes((z - d + n_z) % n_z if sender else z)
        block = ref.at[pl.ds(h * sub, sub), where]
        return remote(block, block, a_send.at[k, h, d - 1], a_recv.at[k, h, d - 1], z_peers[d - 1])

    def out_copy(k, n):
        rows_there = pl.ds(pl.multiple_of(plane_of[n] * rows, rows), rows)
        return remote(
            turned.at[k, rows_there, :], pieces.at[k, n], o_send.at[k, n], o_recv.at[k, n], plane_peers[n]
        )

    def turn(k, value):
        turned[k, :, pl.ds(0, quarter)] = value.T
        for n in range(3):
            out_copy(k, n).start()

    def assemble(k):
        for n in range(3):
            out_copy(k, n).wait_recv()
        found = [turned[k, own_rows, :]] + [pieces[k, n] for n in range(3)]
        if k == seps:
            found = [found[n] + root_pieces[n] for n in range(4)]
        own, by_core, by_y, by_far = (block[:, :quarter] for block in found)
        low_y, low_core = y == 0, c == 0
        same = (jnp.where(low_y, own, by_y), jnp.where(low_y, by_y, own))
        other = (jnp.where(low_y, by_core, by_far), jnp.where(low_y, by_far, by_core))
        blocks = [jnp.where(low_core, same[n], other[n]) for n in range(2)]
        blocks += [jnp.where(low_core, other[n], same[n]) for n in range(2)]
        return jnp.concatenate(blocks, axis=1)

    def join():
        weight_ready(ri_at)
        g_m[:, my_lanes] = dot3(split(g_ri[...]), split(g_q[...]), NN)
        for n in range(3):
            product_copy(n).start()
        weight_ready(rr_at)
        for q in range(2):
            core_copy(0, q).wait_send()
        part[0, :, pl.ds(0, zrows)] = g_rr[...].T
        rr_full[:, zlanes] = part[0, rr_cols, pl.ds(0, zrows)]
        for d in range(1, n_z):
            rr_along_z(d, False).start()

    def rr_along_z(d, sender):
        block = rr_full.at[:, z_lanes((z - d + n_z) % n_z if sender else z)]
        return remote(block, block, r_send.at[d - 1], r_recv.at[d - 1], z_peers[d - 1])

    def wait_along_z(ref, k, h):
        for d in range(1, n_z):
            along_z(ref, k, h, d, True).wait_recv()

    def send_along_z(ref, k, h):
        for d in range(1, n_z):
            along_z(ref, k, h, d, False).start()

    def chain(k, h):
        where = pl.ds(h * sub, sub)
        if h == 0:
            weight_ready(inv_at + k)
            if k > 0:
                weight_ready(chain_at + k - 1)
        value = dot3(split(total[k, where, :]), split(g_inv[k]), NT)
        if k > 0:
            wait_along_z(solved.at[k - 1], k - 1, h)
            value = value - dot3(split(solved[k - 1, where, :]), split(g_chain[k - 1]), NT)
        solved[k, where, zlanes] = value
        send_along_z(solved.at[k], k, h)
        if h == HALVES - 1:
            turn(k, solved[k, :, zlanes])

    stage_a(0)
    stage_a(1)
    stage_b(0)
    send_weights(1)
    for k in range(2, seps):
        stage_a(k)
        stage_b(k - 1)
        send_weights(k)
    stage_b(last)
    send_weights(seps)
    own_quarter.wait()
    for n in range(3):
        quarter_copy(n).wait_recv()
    quarter_round(0)
    order = [numbers[n] for place in PLAN for n in place]
    for n in order:
        weight(1, n).start()
    chunks = [(k, h) for k in range(seps) for h in range(HALVES)]
    last_step = len(chunks) + LAG * (n_z - 1)
    relays, clock = {}, -1 - 2 * len(PLAN[0]) / 3
    for place, numbered in enumerate(PLAN):
        for n in numbered:
            clock += 2 / 3
            relays.setdefault(max(1, math.ceil(clock)), []).append(numbers[n])
        clock += HALVES if place < seps else 0
    chains = {}
    for j, (k, h) in enumerate(chunks):
        chains.setdefault(j + LAG * (n_z - 1) + SHIFT[min(k, 3)], []).append((k, h))

    for step in range(max(last_step, max(chains) + 1, JOIN + 1)):
        for n in relays.pop(step, []):
            relay(n)
        for number in reversed(range(n_z - 1)):
            j = step - LAG * number
            if 0 <= j < len(chunks):
                if number == 0:
                    stage_c(*chunks[j])
                hop(*chunks[j], number)
        j = step - LAG * (n_z - 1)
        if 0 <= j < len(chunks):
            finish(*chunks[j])
        for k, h in chains.get(step, []):
            chain(k, h)
        if step in ROUNDS[: n_z - 1]:
            quarter_round(1 + ROUNDS.index(step))
        if step == JOIN:
            join()
    for step in sorted(relays):
        for n in relays[step]:
            relay(n)

    for k in range(last):
        sep_out[k] = assemble(k)
    for d in range(1, n_z):
        rr_along_z(d, True).wait_recv()
    rr_out[...] = jnp.zeros_like(rr_out)
    rr_out[pl.ds(pl.multiple_of(share * layer, 8), share), :] = dot3(split(rr_full[...]), split(g_ri[...]), NT)
    for n in range(3):
        product_copy(n).wait_recv()
    product = split(g_m[...])
    for h in range(HALVES):
        where = pl.ds(h * sub, sub)
        wait_along_z(solved.at[last], last, h)
        rr_out[where, :] = rr_out[where, :] - dot3(split(solved[last, where, :]), product, NT)

    others = [(1 - layer, me + p - plane) for p in (plane,) + plane_of]

    def cross_copy(n):
        rows_there = pl.ds(pl.multiple_of(((plane,) + plane_of)[n] * rows, rows), rows)
        return remote(
            turned.at[seps, rows_there, :], root_pieces.at[n], x_send.at[n], x_recv.at[n], others[n]
        )

    turned[seps, :, pl.ds(0, quarter)] = rr_out[...].T
    for n in (3, 2, 1, 0):
        cross_copy(n).start()
    for n in range(3):
        out_copy(seps, n).start()
    sep_out[last] = assemble(last)
    for n in range(4):
        cross_copy(n).wait_recv()
    root_out[...] = assemble(seps)
    for k in range(1, seps):
        for q in range(2):
            core_copy(k, q).wait_send()
    ends = [
        pltpu.make_async_copy(sep_out, sep_final, end.at[0]),
        pltpu.make_async_copy(root_out, root_final, end.at[1]),
    ]
    for copy in ends:
        copy.start()

    for way in range(3):
        for n in range(len(weights)):
            weight(way, n).wait_send()
    for k, h in chunks:
        y_copy(k, h).wait_send()

        @pl.when(z < n_z - 1)
        def _():
            fwd_copy(k, h).wait_send()

        @pl.when(z > 0)
        def _():
            bwd_copy(k, h).wait_send()

    for k in range(seps):
        for h in range(HALVES):
            for d in range(1, n_z):
                along_z(solved.at[k], k, h, d, False).wait_send()
    for k in range(seps + 1):
        for n in range(3):
            out_copy(k, n).wait_send()
    for n in range(4):
        cross_copy(n).wait_send()
    for n in range(3):
        quarter_copy(n).wait_send()
        product_copy(n).wait_send()
    for d in range(1, n_z):
        rr_along_z(d, False).wait_send()
    for number in range(n_z - 1):
        for side in range(2):

            @pl.when(gives(side, number))
            def _():
                quarter_hop(side, number, True).wait_send()

    for copy in ends:
        copy.wait()


def keep_out(a):
    return pltpu.with_memory_space_constraint(a, pltpu.HBM)


def fused(
    n_z,
    leaf_rhs,
    leaf_inverse,
    leaf_coupling,
    parent,
    sep_rhs,
    sep_inverse,
    sep_coupling,
    root_coupling,
    root_rhs,
    root_inverse,
):
    seps, rows, right = sep_rhs.shape[1:]
    width = sep_inverse.shape[3]
    deep = leaf_inverse.shape[3]
    zrows, half, quarter = width // n_z, right // 2, right // 4
    f32 = jnp.float32
    dma = pltpu.SemaphoreType.DMA
    vmem = pl.BlockSpec(memory_space=pltpu.VMEM)
    hbm = pl.BlockSpec(memory_space=pltpu.HBM)
    scratch = [
        (seps, rows, right),
        (rows, right),
        (deep, right),
        (deep, deep),
        (seps, width, deep),
        (seps, rows, right),
        (seps, zrows, width),
        (seps - 1, zrows, width),
        (zrows, width),
        (width, width // 4),
        (zrows, right),
        (zrows, width),
        (seps, right, width),
        (seps, half, width),
    ]
    scratch += [(seps, quarter, width)] * 9
    scratch += [
        (zrows, right),
        (seps + 1, zrows, 128),
        (seps + 1, 3, rows, 128),
        (quarter // 2, width),
        (quarter, zrows),
        (4, rows, 128),
    ]
    n_w = 2 * seps + 1
    sems = [(4 + seps,), (n_w,)]
    sems += [(3, n_w)] * 2 + [(seps, 2)] * 2 + [(seps, HALVES)] * 6
    sems += [(seps, HALVES, n_z - 1)] * 2 + [(seps + 1, 3)] * 2 + [(4,)] * 2
    sems += [(3,)] * 4 + [(2, n_z - 1)] * 2 + [(n_z - 1,)] * 2 + [(2,)]
    sep, root = pl.pallas_call(
        functools.partial(kernel, n_z),
        out_shape=(
            jax.ShapeDtypeStruct((seps, rows, right), f32),
            jax.ShapeDtypeStruct((rows, right), f32),
        ),
        in_specs=[pl.BlockSpec(memory_space=pltpu.SMEM)] + [hbm] * 9,
        out_specs=(pl.BlockSpec(memory_space=pl.ANY),) * 2,
        scratch_shapes=[pltpu.VMEM(s, f32) for s in scratch] + [dma(s) for s in sems],
        compiler_params=pltpu.CompilerParams(
            collective_id=0, has_side_effects=True, vmem_limit_bytes=24 * 2**20
        ),
        name="forward_solve",
    )(
        parent,
        *map(keep_out, (
        leaf_rhs.reshape(leaf_rhs.shape[2:]),
        leaf_inverse.reshape(leaf_inverse.shape[2:]),
        leaf_coupling.reshape(leaf_coupling.shape[2:]),
        sep_rhs.reshape(sep_rhs.shape[1:]),
        sep_inverse.reshape(sep_inverse.shape[1:]),
        sep_coupling.reshape(sep_coupling.shape[1:]),
        root_coupling.reshape(root_coupling.shape[1:]),
        root_rhs,
        root_inverse,
        )),
    )
    return write_out(sep, root)


def write(sep, root, sep_out, root_out):
    sep_out[...] = sep[...]
    root_out[...] = root[...]


def write_out(sep, root):
    vmem = pl.BlockSpec(memory_space=pltpu.VMEM)
    shapes = tuple(jax.ShapeDtypeStruct(a.shape, a.dtype) for a in (sep, root))
    sep, root = pl.pallas_call(
        write,
        out_shape=shapes,
        in_specs=[vmem, vmem],
        out_specs=(vmem, vmem),
        compiler_params=pltpu.CompilerParams(vmem_limit_bytes=2 * 2**20),
        name="write_out",
    )(sep, root)
    return sep[None], root


def body(
    leaf_rhs,
    leaf_inverse,
    leaf_coupling,
    parent,
    sep_rhs,
    sep_inverse,
    sep_coupling,
    root_coupling,
    root_rhs,
    root_inverse,
):
    highest = lax.Precision.HIGHEST
    sep_count = sep_rhs.shape[1]
    row_count = sep_rhs.shape[2]
    row_start = lax.axis_index("row") * row_count
    leaf_solution = jnp.dot(leaf_inverse[0, 0], leaf_rhs[0, 0], precision=highest)
    levels = jnp.arange(sep_count, dtype=jnp.int32)
    keep_mask = (levels >= parent[0, 0]).astype(jnp.float32)

    def residual_term(k):
        coupled = jnp.dot(leaf_coupling[0, 0, k], leaf_solution, precision=highest) * keep_mask[k]
        own_rhs = lax.dynamic_update_slice_in_dim(
            jnp.zeros_like(coupled), sep_rhs[0, k], row_start, 0
        )
        return own_rhs - coupled

    residual_list = [lax.psum(residual_term(k), "row") for k in range(sep_count)]
    local_rows = [
        jnp.dot(sep_inverse[0, k], residual_list[k], precision=highest) for k in range(sep_count)
    ]
    solved = []
    gathered = None
    for k in range(sep_count):
        current = local_rows[k]
        if k > 0:
            current = current - jnp.dot(sep_coupling[0, k - 1], gathered, precision=highest)
        solved.append(current)
        gathered = lax.all_gather(current, "row", axis=0, tiled=True)
    sep_out = jnp.stack(solved)[None]
    root_term = jnp.dot(root_coupling[0], gathered, precision=highest)
    root_sum = lax.psum(root_term, "layer")
    root_residual = root_rhs - root_sum
    root_out = jnp.dot(
        root_inverse, lax.all_gather(root_residual, "row", axis=0, tiled=True), precision=highest
    )
    return (sep_out, root_out)


def solution(mesh):
    n_layer, n_row = mesh.shape["layer"], mesh.shape["row"]

    def per_device(*arrays):
        right, width = arrays[0].shape[3], arrays[5].shape[3]
        n_z = n_row // 4
        fits = (
            n_layer == 2
            and n_row in (8, 16)
            and width % 512 == 0
            and width % (128 * n_z) == 0
            and right % (32 * HALVES) == 0
            and right % 64 == 0
            and right // 4 <= 128
            and arrays[4].shape[1] == 4
        )
        return functools.partial(fused, n_z)(*arrays) if fits else body(*arrays)

    return jax.shard_map(
        per_device,
        mesh=mesh,
        in_specs=(
            P("layer", "row", None, None),
            P("layer", "row", None, None),
            P("layer", "row", None, None, None),
            P("layer", "row"),
            P("layer", None, "row", None),
            P("layer", None, "row", None),
            P("layer", None, "row", None),
            P("layer", "row", None),
            P("row", None),
            P("row", None),
        ),
        out_specs=(P("layer", None, "row", None), P("row", None)),
        check_vma=False,
    )
```

```python
import functools
import math

import jax
import jax.numpy as jnp
from jax import lax
from jax.experimental import pallas as pl
from jax.experimental.pallas import tpu as pltpu
from jax.sharding import PartitionSpec as P

MESH = pl.DeviceIdType.MESH
NN = (((1,), (0,)), ((), ()))
NT = (((1,), (1,)), ((), ()))
HALVES = 2
LAG = 2
PLAN = ((0,), (), (1,), (4,), (2, 5, 3, 6, 9, 8))
SHIFT = (0, 0, 1, 3)
JOIN = 12
ROUNDS = (1, 3, 5)


def split(a):
    high = a.astype(jnp.bfloat16)
    return high, (a - high.astype(jnp.float32)).astype(jnp.bfloat16)


def dot3(a, b, dims):
    (ah, al), (bh, bl) = a, b
    dot = functools.partial(lax.dot_general, dimension_numbers=dims, preferred_element_type=jnp.float32)
    return dot(ah, bh) + (dot(ah, bl) + dot(al, bh))


def kernel(
    n_z,
    parent,
    leaf_rhs,
    leaf_inverse,
    leaf_coupling,
    sep_rhs,
    sep_inverse,
    sep_coupling,
    root_coupling,
    root_rhs,
    root_inverse,
    sep_final,
    root_final,
    sep_out,
    root_out,
    v_rhs,
    v_inv,
    v_coup,
    v_sep,
    g_inv,
    g_chain,
    g_m,
    g_q,
    g_rr,
    g_ri,
    part,
    from_core,
    to_y,
    from_y,
    mine,
    fwd,
    bwd,
    from_left,
    from_right,
    total,
    solved,
    padded,
    turned,
    pieces,
    rr_full,
    rr_out,
    root_pieces,
    load,
    own_load,
    w_send,
    w_recv,
    c_send,
    c_recv,
    y_send,
    y_recv,
    f_send,
    f_recv,
    b_send,
    b_recv,
    a_send,
    a_recv,
    o_send,
    o_recv,
    x_send,
    x_recv,
    q_send,
    q_recv,
    m_send,
    m_recv,
    qz_send,
    qz_recv,
    r_send,
    r_recv,
    end,
):
    seps, rows, right = v_sep.shape
    width = v_coup.shape[1]
    zrows = width // n_z
    half, quarter = right // 2, right // 4
    sub = quarter // HALVES
    last = seps - 1

    layer = lax.axis_index("layer")
    me = lax.axis_index("row")
    z, y, c = me // 4, (me // 2) % 2, me % 2
    plane = 2 * y + c

    def at(zz, yy, cc):
        return (layer, 4 * zz + 2 * yy + cc)

    core_peer = at(z, y, 1 - c)
    y_peer = at(z, 1 - y, c)
    far_peer = at(z, 1 - y, 1 - c)
    x_peer = (1 - layer, me)
    lanes = width // 4
    left, right_peer = (layer, me - 4), (layer, me + 4)
    z_peers = [at((z + d) % n_z, y, c) for d in range(1, n_z)]
    plane_peers = [core_peer, y_peer, far_peer]

    def remote(src, dst, send, recv, peer):
        return pltpu.make_async_remote_copy(
            src_ref=src, dst_ref=dst, send_sem=send, recv_sem=recv, device_id=peer, device_id_type=MESH
        )

    barrier = pltpu.get_barrier_semaphore()
    near = plane_peers + [x_peer]
    for peer in near:
        pl.semaphore_signal(barrier, inc=1, device_id=peer, device_id_type=MESH)

    @pl.when(z > 0)
    def _():
        pl.semaphore_signal(barrier, inc=1, device_id=left, device_id_type=MESH)

    @pl.when(z < n_z - 1)
    def _():
        pl.semaphore_signal(barrier, inc=1, device_id=right_peer, device_id_type=MESH)

    def enter():
        pl.semaphore_wait(barrier, len(near) + jnp.minimum(z, 1) + jnp.minimum(n_z - 1 - z, 1))


    own_rows = pl.ds(pl.multiple_of(plane * rows, rows), rows)
    y_rows = pl.ds(pl.multiple_of((2 * (1 - y) + c) * rows, rows), rows)
    weights = [(sep_inverse.at[k], g_inv.at[k]) for k in range(seps)]
    weights += [(sep_coupling.at[k], g_chain.at[k]) for k in range(last)]
    weights += [(root_rhs, g_rr), (root_inverse, g_ri)]
    inv_at, chain_at, rr_at, ri_at = 0, seps, seps + last, seps + last + 1

    loads = [
        pltpu.make_async_copy(leaf_inverse, v_inv, load.at[0]),
        pltpu.make_async_copy(leaf_rhs, v_rhs, load.at[1]),
        pltpu.make_async_copy(sep_rhs, v_sep, load.at[2]),
    ]
    loads += [pltpu.make_async_copy(leaf_coupling.at[k], v_coup.at[k], load.at[3 + k]) for k in range(seps)]
    for n in (0, 1, 3, 2) + tuple(range(4, 3 + seps)):
        loads[n].start()
    own_loads = [
        pltpu.make_async_copy(source, dest.at[own_rows, :], own_load.at[n])
        for n, (source, dest) in enumerate(weights)
    ]
    my_lanes = pl.ds(pl.multiple_of(plane * lanes, 128), lanes)
    q_rows = pl.ds(pl.multiple_of(z * zrows + plane * rows, rows), rows)
    z_rows = pl.ds(pl.multiple_of(z * zrows, rows), zrows)
    own_quarter = pltpu.make_async_copy(root_coupling.at[:, my_lanes], g_q.at[q_rows, :], load.at[3 + seps])
    for copy in own_loads + [own_quarter]:
        copy.start()

    plane_of = (2 * y + 1 - c, 2 * (1 - y) + c, 2 * (1 - y) + 1 - c)

    def quarter_copy(n):
        there = pl.ds(pl.multiple_of(plane_of[n] * lanes, 128), lanes)
        return remote(
            root_coupling.at[:, there], g_q.at[q_rows, :], q_send.at[n], q_recv.at[n], plane_peers[n]
        )

    def quarter_hop(side, number, sent):
        owner = (z - number, z + number)[side] if sent else (z - 1 - number, z + 1 + number)[side]
        block = g_q.at[pl.ds(pl.multiple_of(owner * zrows, rows), zrows), :]
        return remote(
            block, block, qz_send.at[side, number], qz_recv.at[side, number], (right_peer, left)[side]
        )

    def takes(side, number):
        return (z - 1 - number >= 0, z + 1 + number < n_z)[side]

    def gives(side, number):
        far = (z - number >= 0, z + number < n_z)[side]
        return jnp.logical_and(far, (z < n_z - 1, z > 0)[side])

    def quarter_round(number):
        for side in range(2):
            if number > 0:

                @pl.when(takes(side, number - 1))
                def _():
                    quarter_hop(side, number - 1, False).wait_recv()

            if number < n_z - 1:

                @pl.when(gives(side, number))
                def _():
                    quarter_hop(side, number, True).start()

    def product_copy(n):
        return remote(
            g_m.at[:, my_lanes], g_m.at[:, my_lanes], m_send.at[n], m_recv.at[n], plane_peers[n]
        )

    def send_weights(place):
        for n in PLAN[place]:
            weight(0, numbers[n]).start()

    numbers = tuple(range(seps + last)) + (None, rr_at, ri_at)

    def weight(way, n):
        source, dest = weights[n]
        if way == 2:
            source, where = dest.at[y_rows, :], y_rows
        else:
            where = own_rows
        return remote(
            source,
            dest.at[where, :],
            w_send.at[way, n],
            w_recv.at[way, n],
            y_peer if way == 0 else core_peer,
        )

    relayed = set()

    def relay(n):
        if n not in relayed:
            relayed.add(n)
            weight(0, n).wait_recv()
            weight(2, n).start()

    def weight_ready(n):
        relay(n)
        own_loads[n].wait()
        weight(1, n).wait_recv()
        weight(2, n).wait_recv()

    zlanes = pl.ds(pl.multiple_of(z * zrows, 128), zrows)
    own_y = pl.multiple_of(quarter * y, 8)
    peer_y = pl.multiple_of(quarter * (1 - y), 8)
    padded[...] = jnp.zeros_like(padded)

    def core_copy(k, q):
        there = (peer_y, own_y)[q]
        return remote(
            part.at[k, pl.ds(pl.multiple_of(half * (1 - c) + there, 8), quarter), :],
            from_core.at[k, pl.ds(there, quarter), :],
            c_send.at[k, q],
            c_recv.at[k, q],
            core_peer,
        )

    loads[0].wait()
    loads[1].wait()
    leaf = dot3(split(v_inv[...]), split(v_rhs[...]), NN)
    leaf_t = split(leaf.T)

    share = quarter // 2
    rr_start = pl.multiple_of(half * c + quarter * y + share * layer, 8)
    rr_cols = pl.ds(rr_start, share)

    def stage_a(k):
        keep = jnp.where(parent[0, 0] <= k, -1.0, 0.0).astype(jnp.float32)
        loads[3 + k].wait()
        part[k] = dot3(leaf_t, split(v_coup[k]), NT) * keep
        if k == 0:
            loads[2].wait()
        padded[own_rows, :] = v_sep[k]
        part[k, :, zlanes] += padded[...].T
        if k == 0:
            enter()
            for n in range(3):
                quarter_copy(n).start()
            send_weights(0)
        for q in range(2):
            core_copy(k, q).start()

    def y_copy(k, h):
        where = pl.ds(h * sub, sub)
        return remote(
            to_y.at[k, where, :], from_y.at[k, where, :], y_send.at[k, h], y_recv.at[k, h], y_peer
        )

    def stage_b(k):
        core_copy(k, 0).wait_recv()
        to_y[k] = (
            part[k, pl.ds(pl.multiple_of(half * c + peer_y, 8), quarter), :]
            + from_core[k, pl.ds(peer_y, quarter), :]
        )
        for h in range(HALVES):
            y_copy(k, h).start()

    def fwd_copy(k, h):
        where = pl.ds(h * sub, sub)
        return remote(
            fwd.at[k, where, :], from_left.at[k, where, :], f_send.at[k, h], f_recv.at[k, h], right_peer
        )

    def bwd_copy(k, h):
        where = pl.ds(h * sub, sub)
        return remote(
            bwd.at[k, where, :], from_right.at[k, where, :], b_send.at[k, h], b_recv.at[k, h], left
        )

    def stage_c(k, h):
        where = pl.ds(h * sub, sub)
        if h == 0:
            core_copy(k, 1).wait_recv()
        y_copy(k, h).wait_recv()
        mine[k, where, :] = (
            part[k, pl.ds(pl.multiple_of(half * c + own_y + h * sub, 8), sub), :]
            + from_core[k, pl.ds(pl.multiple_of(own_y + h * sub, 8), sub), :]
            + from_y[k, where, :]
        )

    def hop(k, h, number):
        where = pl.ds(h * sub, sub)

        @pl.when(z == number)
        def _():
            if number == 0:
                fwd[k, where, :] = mine[k, where, :]
            else:
                fwd_copy(k, h).wait_recv()
                fwd[k, where, :] = mine[k, where, :] + from_left[k, where, :]
            fwd_copy(k, h).start()

        @pl.when(z == n_z - 1 - number)
        def _():
            if number == 0:
                bwd[k, where, :] = mine[k, where, :]
            else:
                bwd_copy(k, h).wait_recv()
                bwd[k, where, :] = mine[k, where, :] + from_right[k, where, :]
            bwd_copy(k, h).start()

    def finish(k, h):
        where = pl.ds(h * sub, sub)

        @pl.when(z == 0)
        def _():
            bwd_copy(k, h).wait_recv()
            total[k, where, :] = mine[k, where, :] + from_right[k, where, :]

        @pl.when(z == n_z - 1)
        def _():
            fwd_copy(k, h).wait_recv()
            total[k, where, :] = mine[k, where, :] + from_left[k, where, :]

        @pl.when(jnp.logical_and(z > 0, z < n_z - 1))
        def _():
            total[k, where, :] = mine[k, where, :] + (from_left[k, where, :] + from_right[k, where, :])

    def z_lanes(zz):
        return pl.ds(pl.multiple_of(zz * zrows, 128), zrows)

    def along_z(ref, k, h, d, sender):
        where = z_lanes((z - d + n_z) % n_z if sender else z)
        block = ref.at[pl.ds(h * sub, sub), where]
        return remote(block, block, a_send.at[k, h, d - 1], a_recv.at[k, h, d - 1], z_peers[d - 1])

    def out_copy(k, n):
        rows_there = pl.ds(pl.multiple_of(plane_of[n] * rows, rows), rows)
        return remote(
            turned.at[k, rows_there, :], pieces.at[k, n], o_send.at[k, n], o_recv.at[k, n], plane_peers[n]
        )

    def turn(k, value):
        turned[k, :, pl.ds(0, quarter)] = value.T
        for n in range(3):
            out_copy(k, n).start()

    def assemble(k):
        for n in range(3):
            out_copy(k, n).wait_recv()
        found = [turned[k, own_rows, :]] + [pieces[k, n] for n in range(3)]
        if k == seps:
            found = [found[n] + root_pieces[n] for n in range(4)]
        own, by_core, by_y, by_far = (block[:, :quarter] for block in found)
        low_y, low_core = y == 0, c == 0
        same = (jnp.where(low_y, own, by_y), jnp.where(low_y, by_y, own))
        other = (jnp.where(low_y, by_core, by_far), jnp.where(low_y, by_far, by_core))
        blocks = [jnp.where(low_core, same[n], other[n]) for n in range(2)]
        blocks += [jnp.where(low_core, other[n], same[n]) for n in range(2)]
        return jnp.concatenate(blocks, axis=1)

    def join():
        weight_ready(ri_at)
        g_m[:, my_lanes] = dot3(split(g_ri[...]), split(g_q[...]), NN)
        for n in range(3):
            product_copy(n).start()
        weight_ready(rr_at)
        for q in range(2):
            core_copy(0, q).wait_send()
        part[0, :, pl.ds(0, zrows)] = g_rr[...].T
        rr_full[:, zlanes] = part[0, rr_cols, pl.ds(0, zrows)]
        for d in range(1, n_z):
            rr_along_z(d, False).start()

    def rr_along_z(d, sender):
        block = rr_full.at[:, z_lanes((z - d + n_z) % n_z if sender else z)]
        return remote(block, block, r_send.at[d - 1], r_recv.at[d - 1], z_peers[d - 1])

    def wait_along_z(ref, k, h):
        for d in range(1, n_z):
            along_z(ref, k, h, d, True).wait_recv()

    def send_along_z(ref, k, h):
        for at_z in range(n_z):

            @pl.when(z == at_z)
            def _():
                for d in sorted(range(1, n_z), key=lambda d: -abs((at_z + d) % n_z - at_z)):
                    along_z(ref, k, h, d, False).start()

    def chain(k, h):
        where = pl.ds(h * sub, sub)
        if h == 0:
            weight_ready(inv_at + k)
            if k > 0:
                weight_ready(chain_at + k - 1)
        value = dot3(split(total[k, where, :]), split(g_inv[k]), NT)
        if k > 0:
            wait_along_z(solved.at[k - 1], k - 1, h)
            value = value - dot3(split(solved[k - 1, where, :]), split(g_chain[k - 1]), NT)
        solved[k, where, zlanes] = value
        send_along_z(solved.at[k], k, h)
        if h == HALVES - 1:
            turn(k, solved[k, :, zlanes])

    stage_a(0)
    stage_a(1)
    stage_b(0)
    send_weights(1)
    for k in range(2, seps):
        stage_a(k)
        stage_b(k - 1)
        send_weights(k)
    stage_b(last)
    send_weights(seps)
    own_quarter.wait()
    for n in range(3):
        quarter_copy(n).wait_recv()
    quarter_round(0)
    order = [numbers[n] for place in PLAN for n in place]
    for n in order:
        weight(1, n).start()
    chunks = [(k, h) for k in range(seps) for h in range(HALVES)]
    last_step = len(chunks) + LAG * (n_z - 1)
    relays, clock = {}, -1 - HALVES * len(PLAN[0]) / 3
    for place, numbered in enumerate(PLAN):
        for n in numbered:
            clock += HALVES / 3
            relays.setdefault(max(1, math.ceil(clock)), []).append(numbers[n])
        clock += HALVES if place < seps else 0
    chains = {}
    for j, (k, h) in enumerate(chunks):
        chains.setdefault(j + LAG * (n_z - 1) + SHIFT[min(k, 3)], []).append((k, h))

    for step in range(max(last_step, max(chains) + 1, JOIN + 1)):
        for n in relays.pop(step, []):
            relay(n)
        for number in reversed(range(n_z - 1)):
            j = step - LAG * number
            if 0 <= j < len(chunks):
                if number == 0:
                    stage_c(*chunks[j])
                hop(*chunks[j], number)
        j = step - LAG * (n_z - 1)
        if 0 <= j < len(chunks):
            finish(*chunks[j])
        for k, h in chains.get(step, []):
            chain(k, h)
        if step in ROUNDS[: n_z - 1]:
            quarter_round(1 + ROUNDS.index(step))
        if step == JOIN:
            join()
    for step in sorted(relays):
        for n in relays[step]:
            relay(n)

    for k in range(last):
        sep_out[k] = assemble(k)
    for d in range(1, n_z):
        rr_along_z(d, True).wait_recv()
    rr_out[...] = jnp.zeros_like(rr_out)
    rr_out[pl.ds(pl.multiple_of(share * layer, 8), share), :] = dot3(split(rr_full[...]), split(g_ri[...]), NT)
    for n in range(3):
        product_copy(n).wait_recv()
    product = split(g_m[...])
    for h in range(HALVES):
        where = pl.ds(h * sub, sub)
        wait_along_z(solved.at[last], last, h)
        rr_out[where, :] = rr_out[where, :] - dot3(split(solved[last, where, :]), product, NT)

    others = [(1 - layer, me + p - plane) for p in (plane,) + plane_of]

    def cross_copy(n):
        rows_there = pl.ds(pl.multiple_of(((plane,) + plane_of)[n] * rows, rows), rows)
        return remote(
            turned.at[seps, rows_there, :], root_pieces.at[n], x_send.at[n], x_recv.at[n], others[n]
        )

    turned[seps, :, pl.ds(0, quarter)] = rr_out[...].T
    for n in (3, 2, 1, 0):
        cross_copy(n).start()
    for n in range(3):
        out_copy(seps, n).start()
    sep_out[last] = assemble(last)
    for n in range(4):
        cross_copy(n).wait_recv()
    root_out[...] = assemble(seps)
    for k in range(1, seps):
        for q in range(2):
            core_copy(k, q).wait_send()
    ends = [
        pltpu.make_async_copy(sep_out, sep_final, end.at[0]),
        pltpu.make_async_copy(root_out, root_final, end.at[1]),
    ]
    for copy in ends:
        copy.start()

    for way in range(3):
        for n in range(len(weights)):
            weight(way, n).wait_send()
    for k, h in chunks:
        y_copy(k, h).wait_send()

        @pl.when(z < n_z - 1)
        def _():
            fwd_copy(k, h).wait_send()

        @pl.when(z > 0)
        def _():
            bwd_copy(k, h).wait_send()

    for k in range(seps):
        for h in range(HALVES):
            for d in range(1, n_z):
                along_z(solved.at[k], k, h, d, False).wait_send()
    for k in range(seps + 1):
        for n in range(3):
            out_copy(k, n).wait_send()
    for n in range(4):
        cross_copy(n).wait_send()
    for n in range(3):
        quarter_copy(n).wait_send()
        product_copy(n).wait_send()
    for d in range(1, n_z):
        rr_along_z(d, False).wait_send()
    for number in range(n_z - 1):
        for side in range(2):

            @pl.when(gives(side, number))
            def _():
                quarter_hop(side, number, True).wait_send()

    for copy in ends:
        copy.wait()


def keep_out(a):
    return pltpu.with_memory_space_constraint(a, pltpu.HBM)


def fused(
    n_z,
    leaf_rhs,
    leaf_inverse,
    leaf_coupling,
    parent,
    sep_rhs,
    sep_inverse,
    sep_coupling,
    root_coupling,
    root_rhs,
    root_inverse,
):
    seps, rows, right = sep_rhs.shape[1:]
    width = sep_inverse.shape[3]
    deep = leaf_inverse.shape[3]
    zrows, half, quarter = width // n_z, right // 2, right // 4
    f32 = jnp.float32
    dma = pltpu.SemaphoreType.DMA
    vmem = pl.BlockSpec(memory_space=pltpu.VMEM)
    hbm = pl.BlockSpec(memory_space=pltpu.HBM)
    scratch = [
        (seps, rows, right),
        (rows, right),
        (deep, right),
        (deep, deep),
        (seps, width, deep),
        (seps, rows, right),
        (seps, zrows, width),
        (seps - 1, zrows, width),
        (zrows, width),
        (width, width // 4),
        (zrows, right),
        (zrows, width),
        (seps, right, width),
        (seps, half, width),
    ]
    scratch += [(seps, quarter, width)] * 9
    scratch += [
        (zrows, right),
        (seps + 1, zrows, 128),
        (seps + 1, 3, rows, 128),
        (quarter // 2, width),
        (quarter, zrows),
        (4, rows, 128),
    ]
    n_w = 2 * seps + 1
    sems = [(4 + seps,), (n_w,)]
    sems += [(3, n_w)] * 2 + [(seps, 2)] * 2 + [(seps, HALVES)] * 6
    sems += [(seps, HALVES, n_z - 1)] * 2 + [(seps + 1, 3)] * 2 + [(4,)] * 2
    sems += [(3,)] * 4 + [(2, n_z - 1)] * 2 + [(n_z - 1,)] * 2 + [(2,)]
    sep, root = pl.pallas_call(
        functools.partial(kernel, n_z),
        out_shape=(
            jax.ShapeDtypeStruct((seps, rows, right), f32),
            jax.ShapeDtypeStruct((rows, right), f32),
        ),
        in_specs=[pl.BlockSpec(memory_space=pltpu.SMEM)] + [hbm] * 9,
        out_specs=(pl.BlockSpec(memory_space=pl.ANY),) * 2,
        scratch_shapes=[pltpu.VMEM(s, f32) for s in scratch] + [dma(s) for s in sems],
        compiler_params=pltpu.CompilerParams(
            collective_id=0, has_side_effects=True, vmem_limit_bytes=24 * 2**20
        ),
        name="forward_solve",
    )(
        parent,
        *map(keep_out, (
        leaf_rhs.reshape(leaf_rhs.shape[2:]),
        leaf_inverse.reshape(leaf_inverse.shape[2:]),
        leaf_coupling.reshape(leaf_coupling.shape[2:]),
        sep_rhs.reshape(sep_rhs.shape[1:]),
        sep_inverse.reshape(sep_inverse.shape[1:]),
        sep_coupling.reshape(sep_coupling.shape[1:]),
        root_coupling.reshape(root_coupling.shape[1:]),
        root_rhs,
        root_inverse,
        )),
    )
    return write_out(sep, root)


def write(sep, root, sep_out, root_out):
    sep_out[...] = sep[...]
    root_out[...] = root[...]


def write_out(sep, root):
    vmem = pl.BlockSpec(memory_space=pltpu.VMEM)
    shapes = tuple(jax.ShapeDtypeStruct(a.shape, a.dtype) for a in (sep, root))
    sep, root = pl.pallas_call(
        write,
        out_shape=shapes,
        in_specs=[vmem, vmem],
        out_specs=(vmem, vmem),
        compiler_params=pltpu.CompilerParams(vmem_limit_bytes=2 * 2**20),
        name="write_out",
    )(sep, root)
    return sep[None], root


def body(
    leaf_rhs,
    leaf_inverse,
    leaf_coupling,
    parent,
    sep_rhs,
    sep_inverse,
    sep_coupling,
    root_coupling,
    root_rhs,
    root_inverse,
):
    highest = lax.Precision.HIGHEST
    sep_count = sep_rhs.shape[1]
    row_count = sep_rhs.shape[2]
    row_start = lax.axis_index("row") * row_count
    leaf_solution = jnp.dot(leaf_inverse[0, 0], leaf_rhs[0, 0], precision=highest)
    levels = jnp.arange(sep_count, dtype=jnp.int32)
    keep_mask = (levels >= parent[0, 0]).astype(jnp.float32)

    def residual_term(k):
        coupled = jnp.dot(leaf_coupling[0, 0, k], leaf_solution, precision=highest) * keep_mask[k]
        own_rhs = lax.dynamic_update_slice_in_dim(
            jnp.zeros_like(coupled), sep_rhs[0, k], row_start, 0
        )
        return own_rhs - coupled

    residual_list = [lax.psum(residual_term(k), "row") for k in range(sep_count)]
    local_rows = [
        jnp.dot(sep_inverse[0, k], residual_list[k], precision=highest) for k in range(sep_count)
    ]
    solved = []
    gathered = None
    for k in range(sep_count):
        current = local_rows[k]
        if k > 0:
            current = current - jnp.dot(sep_coupling[0, k - 1], gathered, precision=highest)
        solved.append(current)
        gathered = lax.all_gather(current, "row", axis=0, tiled=True)
    sep_out = jnp.stack(solved)[None]
    root_term = jnp.dot(root_coupling[0], gathered, precision=highest)
    root_sum = lax.psum(root_term, "layer")
    root_residual = root_rhs - root_sum
    root_out = jnp.dot(
        root_inverse, lax.all_gather(root_residual, "row", axis=0, tiled=True), precision=highest
    )
    return (sep_out, root_out)


def solution(mesh):
    n_layer, n_row = mesh.shape["layer"], mesh.shape["row"]

    def per_device(*arrays):
        right, width = arrays[0].shape[3], arrays[5].shape[3]
        n_z = n_row // 4
        fits = (
            n_layer == 2
            and n_row in (8, 16)
            and width % 512 == 0
            and width % (128 * n_z) == 0
            and right % (32 * HALVES) == 0
            and right % 64 == 0
            and right // 4 <= 128
            and arrays[4].shape[1] == 4
        )
        return functools.partial(fused, n_z)(*arrays) if fits else body(*arrays)

    return jax.shard_map(
        per_device,
        mesh=mesh,
        in_specs=(
            P("layer", "row", None, None),
            P("layer", "row", None, None),
            P("layer", "row", None, None, None),
            P("layer", "row"),
            P("layer", None, "row", None),
            P("layer", None, "row", None),
            P("layer", None, "row", None),
            P("layer", "row", None),
            P("row", None),
            P("row", None),
        ),
        out_specs=(P("layer", None, "row", None), P("row", None)),
        check_vma=False,
    )
```

```python
import functools
import math

import jax
import jax.numpy as jnp
from jax import lax
from jax.experimental import pallas as pl
from jax.experimental.pallas import tpu as pltpu
from jax.sharding import PartitionSpec as P

MESH = pl.DeviceIdType.MESH
NN = (((1,), (0,)), ((), ()))
NT = (((1,), (1,)), ((), ()))
HALVES = 2
LAG = 2
PLAN = ((0,), (), (1,), (4,), (2, 5, 3, 6, 9, 8))
SHIFT = (0, 0, 1, 2)
JOIN = 12
ROUNDS = (1, 3, 5)


def split(a):
    high = a.astype(jnp.bfloat16)
    return high, (a - high.astype(jnp.float32)).astype(jnp.bfloat16)


def dot3(a, b, dims):
    (ah, al), (bh, bl) = a, b
    dot = functools.partial(lax.dot_general, dimension_numbers=dims, preferred_element_type=jnp.float32)
    return dot(ah, bh) + (dot(ah, bl) + dot(al, bh))


def kernel(
    n_z,
    parent,
    leaf_rhs,
    leaf_inverse,
    leaf_coupling,
    sep_rhs,
    sep_inverse,
    sep_coupling,
    root_coupling,
    root_rhs,
    root_inverse,
    sep_final,
    root_final,
    sep_out,
    root_out,
    v_rhs,
    v_inv,
    v_coup,
    v_sep,
    g_inv,
    g_chain,
    g_m,
    g_q,
    g_rr,
    g_ri,
    part,
    from_core,
    to_y,
    from_y,
    mine,
    fwd,
    bwd,
    from_left,
    from_right,
    total,
    solved,
    padded,
    turned,
    pieces,
    rr_full,
    rr_out,
    root_pieces,
    load,
    own_load,
    w_send,
    w_recv,
    c_send,
    c_recv,
    y_send,
    y_recv,
    f_send,
    f_recv,
    b_send,
    b_recv,
    a_send,
    a_recv,
    o_send,
    o_recv,
    x_send,
    x_recv,
    q_send,
    q_recv,
    m_send,
    m_recv,
    qz_send,
    qz_recv,
    r_send,
    r_recv,
    end,
):
    seps, rows, right = v_sep.shape
    width = v_coup.shape[1]
    zrows = width // n_z
    half, quarter = right // 2, right // 4
    sub = quarter // HALVES
    last = seps - 1

    layer = lax.axis_index("layer")
    me = lax.axis_index("row")
    z, y, c = me // 4, (me // 2) % 2, me % 2
    plane = 2 * y + c

    def at(zz, yy, cc):
        return (layer, 4 * zz + 2 * yy + cc)

    core_peer = at(z, y, 1 - c)
    y_peer = at(z, 1 - y, c)
    far_peer = at(z, 1 - y, 1 - c)
    x_peer = (1 - layer, me)
    lanes = width // 4
    left, right_peer = (layer, me - 4), (layer, me + 4)
    z_peers = [at((z + d) % n_z, y, c) for d in range(1, n_z)]
    plane_peers = [core_peer, y_peer, far_peer]

    def remote(src, dst, send, recv, peer):
        return pltpu.make_async_remote_copy(
            src_ref=src, dst_ref=dst, send_sem=send, recv_sem=recv, device_id=peer, device_id_type=MESH
        )

    barrier = pltpu.get_barrier_semaphore()
    near = plane_peers + [x_peer]
    for peer in near:
        pl.semaphore_signal(barrier, inc=1, device_id=peer, device_id_type=MESH)

    @pl.when(z > 0)
    def _():
        pl.semaphore_signal(barrier, inc=1, device_id=left, device_id_type=MESH)

    @pl.when(z < n_z - 1)
    def _():
        pl.semaphore_signal(barrier, inc=1, device_id=right_peer, device_id_type=MESH)

    def enter():
        pl.semaphore_wait(barrier, len(near) + jnp.minimum(z, 1) + jnp.minimum(n_z - 1 - z, 1))


    own_rows = pl.ds(pl.multiple_of(plane * rows, rows), rows)
    y_rows = pl.ds(pl.multiple_of((2 * (1 - y) + c) * rows, rows), rows)
    weights = [(sep_inverse.at[k], g_inv.at[k]) for k in range(seps)]
    weights += [(sep_coupling.at[k], g_chain.at[k]) for k in range(last)]
    weights += [(root_rhs, g_rr), (root_inverse, g_ri)]
    inv_at, chain_at, rr_at, ri_at = 0, seps, seps + last, seps + last + 1

    loads = [
        pltpu.make_async_copy(leaf_inverse, v_inv, load.at[0]),
        pltpu.make_async_copy(leaf_rhs, v_rhs, load.at[1]),
        pltpu.make_async_copy(sep_rhs, v_sep, load.at[2]),
    ]
    loads += [pltpu.make_async_copy(leaf_coupling.at[k], v_coup.at[k], load.at[3 + k]) for k in range(seps)]
    for n in (0, 1, 3, 2) + tuple(range(4, 3 + seps)):
        loads[n].start()
    own_loads = [
        pltpu.make_async_copy(source, dest.at[own_rows, :], own_load.at[n])
        for n, (source, dest) in enumerate(weights)
    ]
    my_lanes = pl.ds(pl.multiple_of(plane * lanes, 128), lanes)
    q_rows = pl.ds(pl.multiple_of(z * zrows + plane * rows, rows), rows)
    z_rows = pl.ds(pl.multiple_of(z * zrows, rows), zrows)
    own_quarter = pltpu.make_async_copy(root_coupling.at[:, my_lanes], g_q.at[q_rows, :], load.at[3 + seps])
    for copy in own_loads + [own_quarter]:
        copy.start()

    plane_of = (2 * y + 1 - c, 2 * (1 - y) + c, 2 * (1 - y) + 1 - c)

    def quarter_copy(n):
        there = pl.ds(pl.multiple_of(plane_of[n] * lanes, 128), lanes)
        return remote(
            root_coupling.at[:, there], g_q.at[q_rows, :], q_send.at[n], q_recv.at[n], plane_peers[n]
        )

    def quarter_hop(side, number, sent):
        owner = (z - number, z + number)[side] if sent else (z - 1 - number, z + 1 + number)[side]
        block = g_q.at[pl.ds(pl.multiple_of(owner * zrows, rows), zrows), :]
        return remote(
            block, block, qz_send.at[side, number], qz_recv.at[side, number], (right_peer, left)[side]
        )

    def takes(side, number):
        return (z - 1 - number >= 0, z + 1 + number < n_z)[side]

    def gives(side, number):
        far = (z - number >= 0, z + number < n_z)[side]
        return jnp.logical_and(far, (z < n_z - 1, z > 0)[side])

    def quarter_round(number):
        for side in range(2):
            if number > 0:

                @pl.when(takes(side, number - 1))
                def _():
                    quarter_hop(side, number - 1, False).wait_recv()

            if number < n_z - 1:

                @pl.when(gives(side, number))
                def _():
                    quarter_hop(side, number, True).start()

    def product_copy(n):
        return remote(
            g_m.at[:, my_lanes], g_m.at[:, my_lanes], m_send.at[n], m_recv.at[n], plane_peers[n]
        )

    def send_weights(place):
        for n in PLAN[place]:
            weight(0, numbers[n]).start()

    numbers = tuple(range(seps + last)) + (None, rr_at, ri_at)

    def weight(way, n):
        source, dest = weights[n]
        if way == 2:
            source, where = dest.at[y_rows, :], y_rows
        else:
            where = own_rows
        return remote(
            source,
            dest.at[where, :],
            w_send.at[way, n],
            w_recv.at[way, n],
            y_peer if way == 0 else core_peer,
        )

    relayed = set()

    def relay(n):
        if n not in relayed:
            relayed.add(n)
            weight(0, n).wait_recv()
            weight(2, n).start()

    def weight_ready(n):
        relay(n)
        own_loads[n].wait()
        weight(1, n).wait_recv()
        weight(2, n).wait_recv()

    zlanes = pl.ds(pl.multiple_of(z * zrows, 128), zrows)
    own_y = pl.multiple_of(quarter * y, 8)
    peer_y = pl.multiple_of(quarter * (1 - y), 8)
    padded[...] = jnp.zeros_like(padded)

    def core_copy(k, q):
        there = (peer_y, own_y)[q]
        return remote(
            part.at[k, pl.ds(pl.multiple_of(half * (1 - c) + there, 8), quarter), :],
            from_core.at[k, pl.ds(there, quarter), :],
            c_send.at[k, q],
            c_recv.at[k, q],
            core_peer,
        )

    loads[0].wait()
    loads[1].wait()
    leaf = dot3(split(v_inv[...]), split(v_rhs[...]), NN)
    leaf_t = split(leaf.T)

    share = quarter // 2
    rr_start = pl.multiple_of(half * c + quarter * y + share * layer, 8)
    rr_cols = pl.ds(rr_start, share)

    def stage_a(k):
        keep = jnp.where(parent[0, 0] <= k, -1.0, 0.0).astype(jnp.float32)
        loads[3 + k].wait()
        part[k] = dot3(leaf_t, split(v_coup[k]), NT) * keep
        if k == 0:
            loads[2].wait()
        padded[own_rows, :] = v_sep[k]
        part[k, :, zlanes] += padded[...].T
        if k == 0:
            enter()
            for n in range(3):
                quarter_copy(n).start()
            send_weights(0)
        for q in range(2):
            core_copy(k, q).start()

    def y_copy(k, h):
        where = pl.ds(h * sub, sub)
        return remote(
            to_y.at[k, where, :], from_y.at[k, where, :], y_send.at[k, h], y_recv.at[k, h], y_peer
        )

    def stage_b(k):
        core_copy(k, 0).wait_recv()
        to_y[k] = (
            part[k, pl.ds(pl.multiple_of(half * c + peer_y, 8), quarter), :]
            + from_core[k, pl.ds(peer_y, quarter), :]
        )
        for h in range(HALVES):
            y_copy(k, h).start()

    def fwd_copy(k, h):
        where = pl.ds(h * sub, sub)
        return remote(
            fwd.at[k, where, :], from_left.at[k, where, :], f_send.at[k, h], f_recv.at[k, h], right_peer
        )

    def bwd_copy(k, h):
        where = pl.ds(h * sub, sub)
        return remote(
            bwd.at[k, where, :], from_right.at[k, where, :], b_send.at[k, h], b_recv.at[k, h], left
        )

    def stage_c(k, h):
        where = pl.ds(h * sub, sub)
        if h == 0:
            core_copy(k, 1).wait_recv()
        y_copy(k, h).wait_recv()
        mine[k, where, :] = (
            part[k, pl.ds(pl.multiple_of(half * c + own_y + h * sub, 8), sub), :]
            + from_core[k, pl.ds(pl.multiple_of(own_y + h * sub, 8), sub), :]
            + from_y[k, where, :]
        )

    def hop(k, h, number):
        where = pl.ds(h * sub, sub)

        @pl.when(z == number)
        def _():
            if number == 0:
                fwd[k, where, :] = mine[k, where, :]
            else:
                fwd_copy(k, h).wait_recv()
                fwd[k, where, :] = mine[k, where, :] + from_left[k, where, :]
            fwd_copy(k, h).start()

        @pl.when(z == n_z - 1 - number)
        def _():
            if number == 0:
                bwd[k, where, :] = mine[k, where, :]
            else:
                bwd_copy(k, h).wait_recv()
                bwd[k, where, :] = mine[k, where, :] + from_right[k, where, :]
            bwd_copy(k, h).start()

    def finish(k, h):
        where = pl.ds(h * sub, sub)

        @pl.when(z == 0)
        def _():
            bwd_copy(k, h).wait_recv()
            total[k, where, :] = mine[k, where, :] + from_right[k, where, :]

        @pl.when(z == n_z - 1)
        def _():
            fwd_copy(k, h).wait_recv()
            total[k, where, :] = mine[k, where, :] + from_left[k, where, :]

        @pl.when(jnp.logical_and(z > 0, z < n_z - 1))
        def _():
            total[k, where, :] = mine[k, where, :] + (from_left[k, where, :] + from_right[k, where, :])

    def z_lanes(zz):
        return pl.ds(pl.multiple_of(zz * zrows, 128), zrows)

    def along_z(ref, k, h, d, sender):
        where = z_lanes((z - d + n_z) % n_z if sender else z)
        block = ref.at[pl.ds(h * sub, sub), where]
        return remote(block, block, a_send.at[k, h, d - 1], a_recv.at[k, h, d - 1], z_peers[d - 1])

    def out_copy(k, n):
        rows_there = pl.ds(pl.multiple_of(plane_of[n] * rows, rows), rows)
        return remote(
            turned.at[k, rows_there, :], pieces.at[k, n], o_send.at[k, n], o_recv.at[k, n], plane_peers[n]
        )

    def turn(k, value):
        turned[k, :, pl.ds(0, quarter)] = value.T
        for n in range(3):
            out_copy(k, n).start()

    def assemble(k):
        for n in range(3):
            out_copy(k, n).wait_recv()
        found = [turned[k, own_rows, :]] + [pieces[k, n] for n in range(3)]
        if k == seps:
            found = [found[n] + root_pieces[n] for n in range(4)]
        own, by_core, by_y, by_far = (block[:, :quarter] for block in found)
        low_y, low_core = y == 0, c == 0
        same = (jnp.where(low_y, own, by_y), jnp.where(low_y, by_y, own))
        other = (jnp.where(low_y, by_core, by_far), jnp.where(low_y, by_far, by_core))
        blocks = [jnp.where(low_core, same[n], other[n]) for n in range(2)]
        blocks += [jnp.where(low_core, other[n], same[n]) for n in range(2)]
        return jnp.concatenate(blocks, axis=1)

    def join():
        weight_ready(ri_at)
        g_m[:, my_lanes] = dot3(split(g_ri[...]), split(g_q[...]), NN)
        for n in range(3):
            product_copy(n).start()
        weight_ready(rr_at)
        for q in range(2):
            core_copy(0, q).wait_send()
        part[0, :, pl.ds(0, zrows)] = g_rr[...].T
        rr_full[:, zlanes] = part[0, rr_cols, pl.ds(0, zrows)]
        for d in range(1, n_z):
            rr_along_z(d, False).start()

    def rr_along_z(d, sender):
        block = rr_full.at[:, z_lanes((z - d + n_z) % n_z if sender else z)]
        return remote(block, block, r_send.at[d - 1], r_recv.at[d - 1], z_peers[d - 1])

    def wait_along_z(ref, k, h):
        for d in range(1, n_z):
            along_z(ref, k, h, d, True).wait_recv()

    def send_along_z(ref, k, h):
        for at_z in range(n_z):

            @pl.when(z == at_z)
            def _():
                for d in sorted(range(1, n_z), key=lambda d: -abs((at_z + d) % n_z - at_z)):
                    along_z(ref, k, h, d, False).start()

    def chain(k, h):
        where = pl.ds(h * sub, sub)
        if h == 0:
            weight_ready(inv_at + k)
            if k > 0:
                weight_ready(chain_at + k - 1)
        value = dot3(split(total[k, where, :]), split(g_inv[k]), NT)
        if k > 0:
            wait_along_z(solved.at[k - 1], k - 1, h)
            value = value - dot3(split(solved[k - 1, where, :]), split(g_chain[k - 1]), NT)
        solved[k, where, zlanes] = value
        send_along_z(solved.at[k], k, h)
        if h == HALVES - 1:
            turn(k, solved[k, :, zlanes])

    stage_a(0)
    stage_a(1)
    stage_b(0)
    send_weights(1)
    for k in range(2, seps):
        stage_a(k)
        stage_b(k - 1)
        send_weights(k)
    stage_b(last)
    send_weights(seps)
    own_quarter.wait()
    for n in range(3):
        quarter_copy(n).wait_recv()
    quarter_round(0)
    order = [numbers[n] for place in PLAN for n in place]
    for n in order:
        weight(1, n).start()
    chunks = [(k, h) for k in range(seps) for h in range(HALVES)]
    last_step = len(chunks) + LAG * (n_z - 1)
    relays, clock = {}, -1 - HALVES * len(PLAN[0]) / 3
    for place, numbered in enumerate(PLAN):
        for n in numbered:
            clock += HALVES / 3
            relays.setdefault(max(1, math.ceil(clock)), []).append(numbers[n])
        clock += HALVES if place < seps else 0
    chains = {}
    for j, (k, h) in enumerate(chunks):
        chains.setdefault(j + LAG * (n_z - 1) + SHIFT[min(k, 3)], []).append((k, h))

    for step in range(max(last_step, max(chains) + 1, JOIN + 1)):
        for n in relays.pop(step, []):
            relay(n)
        for number in reversed(range(n_z - 1)):
            j = step - LAG * number
            if 0 <= j < len(chunks):
                if number == 0:
                    stage_c(*chunks[j])
                hop(*chunks[j], number)
        j = step - LAG * (n_z - 1)
        if 0 <= j < len(chunks):
            finish(*chunks[j])
        for k, h in chains.get(step, []):
            chain(k, h)
        if step in ROUNDS[: n_z - 1]:
            quarter_round(1 + ROUNDS.index(step))
        if step == JOIN:
            join()
    for step in sorted(relays):
        for n in relays[step]:
            relay(n)

    for k in range(last):
        sep_out[k] = assemble(k)
    early = pltpu.make_async_copy(sep_out.at[pl.ds(0, last)], sep_final.at[pl.ds(0, last)], end.at[2])
    early.start()
    for d in range(1, n_z):
        rr_along_z(d, True).wait_recv()
    rr_out[...] = jnp.zeros_like(rr_out)
    rr_out[pl.ds(pl.multiple_of(share * layer, 8), share), :] = dot3(split(rr_full[...]), split(g_ri[...]), NT)
    for n in range(3):
        product_copy(n).wait_recv()
    product = split(g_m[...])
    for h in range(HALVES):
        where = pl.ds(h * sub, sub)
        wait_along_z(solved.at[last], last, h)
        rr_out[where, :] = rr_out[where, :] - dot3(split(solved[last, where, :]), product, NT)

    others = [(1 - layer, me + p - plane) for p in (plane,) + plane_of]

    def cross_copy(n):
        rows_there = pl.ds(pl.multiple_of(((plane,) + plane_of)[n] * rows, rows), rows)
        return remote(
            turned.at[seps, rows_there, :], root_pieces.at[n], x_send.at[n], x_recv.at[n], others[n]
        )

    turned[seps, :, pl.ds(0, quarter)] = rr_out[...].T
    for n in (3, 2, 1, 0):
        cross_copy(n).start()
    for n in range(3):
        out_copy(seps, n).start()
    sep_out[last] = assemble(last)
    for n in range(4):
        cross_copy(n).wait_recv()
    root_out[...] = assemble(seps)
    for k in range(1, seps):
        for q in range(2):
            core_copy(k, q).wait_send()
    ends = [
        pltpu.make_async_copy(sep_out.at[last], sep_final.at[last], end.at[0]),
        pltpu.make_async_copy(root_out, root_final, end.at[1]),
    ]
    for copy in ends:
        copy.start()

    for way in range(3):
        for n in range(len(weights)):
            weight(way, n).wait_send()
    for k, h in chunks:
        y_copy(k, h).wait_send()

        @pl.when(z < n_z - 1)
        def _():
            fwd_copy(k, h).wait_send()

        @pl.when(z > 0)
        def _():
            bwd_copy(k, h).wait_send()

    for k in range(seps):
        for h in range(HALVES):
            for d in range(1, n_z):
                along_z(solved.at[k], k, h, d, False).wait_send()
    for k in range(seps + 1):
        for n in range(3):
            out_copy(k, n).wait_send()
    for n in range(4):
        cross_copy(n).wait_send()
    for n in range(3):
        quarter_copy(n).wait_send()
        product_copy(n).wait_send()
    for d in range(1, n_z):
        rr_along_z(d, False).wait_send()
    for number in range(n_z - 1):
        for side in range(2):

            @pl.when(gives(side, number))
            def _():
                quarter_hop(side, number, True).wait_send()

    for copy in ends + [early]:
        copy.wait()


def keep_out(a):
    return pltpu.with_memory_space_constraint(a, pltpu.HBM)


def fused(
    n_z,
    leaf_rhs,
    leaf_inverse,
    leaf_coupling,
    parent,
    sep_rhs,
    sep_inverse,
    sep_coupling,
    root_coupling,
    root_rhs,
    root_inverse,
):
    seps, rows, right = sep_rhs.shape[1:]
    width = sep_inverse.shape[3]
    deep = leaf_inverse.shape[3]
    zrows, half, quarter = width // n_z, right // 2, right // 4
    f32 = jnp.float32
    dma = pltpu.SemaphoreType.DMA
    vmem = pl.BlockSpec(memory_space=pltpu.VMEM)
    hbm = pl.BlockSpec(memory_space=pltpu.HBM)
    scratch = [
        (seps, rows, right),
        (rows, right),
        (deep, right),
        (deep, deep),
        (seps, width, deep),
        (seps, rows, right),
        (seps, zrows, width),
        (seps - 1, zrows, width),
        (zrows, width),
        (width, width // 4),
        (zrows, right),
        (zrows, width),
        (seps, right, width),
        (seps, half, width),
    ]
    scratch += [(seps, quarter, width)] * 9
    scratch += [
        (zrows, right),
        (seps + 1, zrows, 128),
        (seps + 1, 3, rows, 128),
        (quarter // 2, width),
        (quarter, zrows),
        (4, rows, 128),
    ]
    n_w = 2 * seps + 1
    sems = [(4 + seps,), (n_w,)]
    sems += [(3, n_w)] * 2 + [(seps, 2)] * 2 + [(seps, HALVES)] * 6
    sems += [(seps, HALVES, n_z - 1)] * 2 + [(seps + 1, 3)] * 2 + [(4,)] * 2
    sems += [(3,)] * 4 + [(2, n_z - 1)] * 2 + [(n_z - 1,)] * 2 + [(3,)]
    sep, root = pl.pallas_call(
        functools.partial(kernel, n_z),
        out_shape=(
            jax.ShapeDtypeStruct((seps, rows, right), f32),
            jax.ShapeDtypeStruct((rows, right), f32),
        ),
        in_specs=[pl.BlockSpec(memory_space=pltpu.SMEM)] + [hbm] * 9,
        out_specs=(pl.BlockSpec(memory_space=pl.ANY),) * 2,
        scratch_shapes=[pltpu.VMEM(s, f32) for s in scratch] + [dma(s) for s in sems],
        compiler_params=pltpu.CompilerParams(
            collective_id=0, has_side_effects=True, vmem_limit_bytes=24 * 2**20
        ),
        name="forward_solve",
    )(
        parent,
        *map(keep_out, (
        leaf_rhs.reshape(leaf_rhs.shape[2:]),
        leaf_inverse.reshape(leaf_inverse.shape[2:]),
        leaf_coupling.reshape(leaf_coupling.shape[2:]),
        sep_rhs.reshape(sep_rhs.shape[1:]),
        sep_inverse.reshape(sep_inverse.shape[1:]),
        sep_coupling.reshape(sep_coupling.shape[1:]),
        root_coupling.reshape(root_coupling.shape[1:]),
        root_rhs,
        root_inverse,
        )),
    )
    return write_out(sep, root)


def write(sep, root, sep_out, root_out):
    sep_out[...] = sep[...]
    root_out[...] = root[...]


def write_out(sep, root):
    vmem = pl.BlockSpec(memory_space=pltpu.VMEM)
    shapes = tuple(jax.ShapeDtypeStruct(a.shape, a.dtype) for a in (sep, root))
    sep, root = pl.pallas_call(
        write,
        out_shape=shapes,
        in_specs=[vmem, vmem],
        out_specs=(vmem, vmem),
        compiler_params=pltpu.CompilerParams(vmem_limit_bytes=2 * 2**20),
        name="write_out",
    )(sep, root)
    return sep[None], root


def body(
    leaf_rhs,
    leaf_inverse,
    leaf_coupling,
    parent,
    sep_rhs,
    sep_inverse,
    sep_coupling,
    root_coupling,
    root_rhs,
    root_inverse,
):
    highest = lax.Precision.HIGHEST
    sep_count = sep_rhs.shape[1]
    row_count = sep_rhs.shape[2]
    row_start = lax.axis_index("row") * row_count
    leaf_solution = jnp.dot(leaf_inverse[0, 0], leaf_rhs[0, 0], precision=highest)
    levels = jnp.arange(sep_count, dtype=jnp.int32)
    keep_mask = (levels >= parent[0, 0]).astype(jnp.float32)

    def residual_term(k):
        coupled = jnp.dot(leaf_coupling[0, 0, k], leaf_solution, precision=highest) * keep_mask[k]
        own_rhs = lax.dynamic_update_slice_in_dim(
            jnp.zeros_like(coupled), sep_rhs[0, k], row_start, 0
        )
        return own_rhs - coupled

    residual_list = [lax.psum(residual_term(k), "row") for k in range(sep_count)]
    local_rows = [
        jnp.dot(sep_inverse[0, k], residual_list[k], precision=highest) for k in range(sep_count)
    ]
    solved = []
    gathered = None
    for k in range(sep_count):
        current = local_rows[k]
        if k > 0:
            current = current - jnp.dot(sep_coupling[0, k - 1], gathered, precision=highest)
        solved.append(current)
        gathered = lax.all_gather(current, "row", axis=0, tiled=True)
    sep_out = jnp.stack(solved)[None]
    root_term = jnp.dot(root_coupling[0], gathered, precision=highest)
    root_sum = lax.psum(root_term, "layer")
    root_residual = root_rhs - root_sum
    root_out = jnp.dot(
        root_inverse, lax.all_gather(root_residual, "row", axis=0, tiled=True), precision=highest
    )
    return (sep_out, root_out)


def solution(mesh):
    n_layer, n_row = mesh.shape["layer"], mesh.shape["row"]

    def per_device(*arrays):
        right, width = arrays[0].shape[3], arrays[5].shape[3]
        n_z = n_row // 4
        fits = (
            n_layer == 2
            and n_row in (8, 16)
            and width % 512 == 0
            and width % (128 * n_z) == 0
            and right % (32 * HALVES) == 0
            and right % 64 == 0
            and right // 4 <= 128
            and arrays[4].shape[1] == 4
        )
        return functools.partial(fused, n_z)(*arrays) if fits else body(*arrays)

    return jax.shard_map(
        per_device,
        mesh=mesh,
        in_specs=(
            P("layer", "row", None, None),
            P("layer", "row", None, None),
            P("layer", "row", None, None, None),
            P("layer", "row"),
            P("layer", None, "row", None),
            P("layer", None, "row", None),
            P("layer", None, "row", None),
            P("layer", "row", None),
            P("row", None),
            P("row", None),
        ),
        out_specs=(P("layer", None, "row", None), P("row", None)),
        check_vma=False,
    )
```
